32 devices in a mesh: groups: 2 (over y), gx: 16 (over z, x, core).
Axes of the slice: x: 2, y: 2, z: 4, core: 2. Of those that a mesh axis runs over, the one named last changes fastest.
Arguments:
- grad_out: bfloat16 [64, 4, 128, 128], P(('groups', 'gx')), parts along dimension 0, may hold values from -6 to 6
- inputs: bfloat16 [64, 4, 128, 128], P(('groups', 'gx')), parts along dimension 0, may hold values from -6 to 6
- pre_first: bfloat16 [64, 4, 128, 128], P(('groups', 'gx')), parts along dimension 0, may hold values from -6 to 6
- pre_second: bfloat16 [64, 4, 128, 128], P(('groups', 'gx')), parts along dimension 0, may hold values from -6 to 6
- filter_first: bfloat16 [3456, 128], P('gx'), may hold values from -0.109375 to 0.109375
- filter_second: bfloat16 [3456, 128], P('gx'), may hold values from -0.109375 to 0.109375
Outputs:
- grad_inputs: bfloat16 [64, 4, 128, 128], P(('groups', 'gx')), parts along dimension 0
- grad_filter_first: float32 [3456, 256], P('gx', 'groups'), parts along dimension 1
- grad_filter_second: float32 [3456, 256], P('gx', 'groups'), parts along dimension 1
The draws below stay inside these ranges and needn't reach their ends.
There are 2 independent parts, one for each index of `groups`. The reference program is written for one: setup_inputs(seed, part) draws one part's arguments, and reference() takes and returns one part's arrays. A program takes and returns all parts, laid end to end along the dimension named above; an argument that names none is the same for every part. Nothing has to cross between parts.
All inputs are finite; a program needn't handle non-finite values.
Results may differ from the reference program's by a relative error of at most 0.0058.
Values may be sent and summed in bfloat16 or wider, within the bound.
A program may use at most 64 MiB of HBM per device.

```python
import math
import jax
import jax.numpy as jnp
from jax import lax

C = 128
Y = 4
Z = 128
NX = 32


def level_of(key, dims, pieces, least, largest):
    level, own = 1.0, jax.random.fold_in(key, 6)
    for position, parts in pieces:
        heights = jnp.exp(jax.random.uniform(jax.random.fold_in(own, position), (parts,), jnp.float32, least / len(pieces), largest / len(pieces)))
        level = level * jnp.repeat(heights, dims[position] // parts).reshape([-1 if axis == position else 1 for axis in range(len(dims))])
    return level


def noise(key, dims, width, most, split=(), dtype=jnp.bfloat16):
    entries = width * jax.random.normal(key, dims, jnp.float32)
    if split:
        entries = entries * level_of(key, dims, split, -0.22, 0.18)
    return jnp.clip(entries, -most, most).astype(dtype)


def setup_inputs(seed: int = 0, part: int = 0) -> dict:
    key_of = jax.random.split(jax.random.key(seed), 7)
    part_splits = jax.random.split(jax.random.fold_in(key_of[6], part), 7)
    return {
        "grad_out": noise(part_splits[0], (NX, Y, Z, C), 1.0, 6.0, ((0, 16),)),
        "inputs": noise(part_splits[1], (NX, Y, Z, C), 1.0, 6.0, ((0, 16),)),
        "pre_first": noise(part_splits[2], (NX, Y, Z, C), 1.0, 6.0, ((0, 16),)),
        "pre_second": noise(part_splits[3], (NX, Y, Z, C), 1.0, 6.0, ((0, 16),)),
        "filter_first": noise(key_of[4], (27 * C, C), (27 * C) ** -0.5, 0.109375, ((0, 16),)),
        "filter_second": noise(key_of[5], (27 * C, C), (27 * C) ** -0.5, 0.109375, ((0, 16),)),
    }


inv_root_two = 0.7071067811865476
inv_root_twopi = 0.3989422804014327

def gelu_parts(value):
    normal_cdf = 0.5 * (1.0 + lax.erf(value * inv_root_two))
    return (value * normal_cdf, normal_cdf + value * jnp.exp(-0.5 * value * value) * inv_root_twopi)

def pad_field(field):
    return jnp.pad(field, ((1, 1), (1, 1), (1, 1), (0, 0)))

def back_data(grads, weights):
    x_cells, y_cells, z_cells, channels = grads.shape
    padded = pad_field(grads.astype(jnp.float32))
    weights = weights.astype(jnp.float32)
    running = jnp.zeros((x_cells * y_cells * z_cells, channels), jnp.float32)
    for shift_a in (-1, 0, 1):
        for shift_b in (-1, 0, 1):
            for shift_c in (-1, 0, 1):
                index = 9 * (shift_a + 1) + 3 * (shift_b + 1) + (shift_c + 1)
                tap = weights[index * channels:(index + 1) * channels]
                piece = padded[1 - shift_a:1 - shift_a + x_cells, 1 - shift_b:1 - shift_b + y_cells, 1 - shift_c:1 - shift_c + z_cells].reshape(-1, channels)
                running = running + jnp.dot(piece, tap.T, precision=lax.Precision.HIGHEST)
    return running.reshape(grads.shape)

def back_filter(saved, grads):
    x_cells, y_cells, z_cells, channels = grads.shape
    padded = pad_field(saved.astype(jnp.float32))
    flat_grads = grads.astype(jnp.float32).reshape(-1, channels)
    blocks = []
    for shift_a in (-1, 0, 1):
        for shift_b in (-1, 0, 1):
            for shift_c in (-1, 0, 1):
                piece = padded[1 + shift_a:1 + shift_a + x_cells, 1 + shift_b:1 + shift_b + y_cells, 1 + shift_c:1 + shift_c + z_cells].reshape(-1, channels)
                blocks.append(jnp.dot(piece.T, flat_grads, precision=lax.Precision.HIGHEST))
    return jnp.concatenate(blocks, axis=0)

def reference(grad_out, inputs, pre_first, pre_second, filter_first, filter_second):
    grad_scale = 1.0 / math.sqrt(NX * Y * Z)
    unused_value, slope_two = gelu_parts(pre_second.astype(jnp.float32))
    grad_two = (grad_out.astype(jnp.float32) * slope_two).astype(jnp.bfloat16)
    act_one, slope_one = gelu_parts(pre_first.astype(jnp.float32))
    act_one = act_one.astype(jnp.bfloat16)
    grad_act = back_data(grad_two, filter_second)
    filt_two = back_filter(act_one, grad_two)
    grad_one = (grad_act * slope_one).astype(jnp.bfloat16)
    grad_in = back_data(grad_one, filter_first)
    filt_one = back_filter(inputs, grad_one)
    return (grad_in.astype(jnp.bfloat16), filt_one * grad_scale, filt_two * grad_scale)
```

```python
import functools
import math

import jax
import jax.numpy as jnp
from jax import lax
from jax.experimental import pallas as pl
from jax.experimental.pallas import tpu as pltpu
from jax.sharding import PartitionSpec as P

inv_root_two = 0.7071067811865476
inv_root_twopi = 0.3989422804014327
tap_shifts = ((-1, -1), (-1, 0), (-1, 1), (0, -1), (0, 0), (0, 1), (1, -1), (1, 0), (1, 1))


def with_halo(block, sides, width):
    for axis, dim in sides:
        count = lax.axis_size(axis)
        forward = [(i, i + 1) for i in range(count - 1)]
        backward = [(target, source) for source, target in forward]
        low = lax.ppermute(
            lax.slice_in_dim(block, block.shape[dim] - width, None, axis=dim), axis, forward
        )
        high = lax.ppermute(lax.slice_in_dim(block, 0, width, axis=dim), axis, backward)
        block = jnp.concatenate([low, block, high], axis=dim)
    return block


def gelu_parts(value):
    normal_cdf = 0.5 * (1.0 + lax.erf(value * inv_root_two))
    return (value * normal_cdf, normal_cdf + value * jnp.exp(-0.5 * value * value) * inv_root_twopi)


def pad_sides(extended):
    return jnp.pad(extended, ((0, 0), (1, 1), (1, 1), (0, 0)))


def stack_taps(padded, direction, z_cells):
    return jnp.concatenate(
        [
            padded[:, :, 1 + direction * shift_z : 1 + direction * shift_z + z_cells]
            for shift_z in (-1, 0, 1)
        ],
        axis=3,
    )


def window(stacked, direction, shift_x, shift_y, x_cells, y_cells):
    start_x = 1 + direction * shift_x
    start_y = 1 + direction * shift_y
    return stacked[start_x : start_x + x_cells, start_y : start_y + y_cells]


def back_data(stacked, full_filter, shape):
    x_cells, y_cells, z_cells, channels = shape
    kernel = full_filter.reshape(3, 3, 3, channels, channels)
    running = jnp.zeros((x_cells * y_cells * z_cells, channels), jnp.float32)
    for shift_x, shift_y in tap_shifts:
        tap_matrix = jnp.transpose(kernel[shift_x + 1, shift_y + 1], (0, 2, 1)).reshape(
            3 * channels, channels
        )
        piece = window(stacked, -1, shift_x, shift_y, x_cells, y_cells).reshape(-1, 3 * channels)
        running = running + jnp.dot(piece, tap_matrix, preferred_element_type=jnp.float32)
    return running.reshape(shape)


def filter_from_inputs(stacked, grads, shape):
    x_cells, y_cells, z_cells, channels = shape
    flat_grads = grads.reshape(-1, channels)
    blocks = []
    for shift_x, shift_y in tap_shifts:
        piece = window(stacked, 1, shift_x, shift_y, x_cells, y_cells).reshape(-1, 3 * channels)
        product = lax.dot_general(
            piece, flat_grads, (((0,), (0,)), ((), ())), preferred_element_type=jnp.float32
        )
        blocks.append(product.reshape(3, channels, channels))
    return jnp.stack(blocks).reshape(27 * channels, channels)


def on_device(grad_out, inputs, pre_first, pre_second, filter_first, filter_second):
    shape = grad_out.shape
    x_cells, y_cells, z_cells, channels = shape
    full_first, full_second = (
        lax.all_gather(filter_first, "gx", axis=0, tiled=True),
        lax.all_gather(filter_second, "gx", axis=0, tiled=True),
    )
    grad_scale = 1.0 / math.sqrt(x_cells * lax.axis_size("gx") * y_cells * z_cells)
    unused_value, slope_two = gelu_parts(pre_second.astype(jnp.float32))
    grad_two = (grad_out.astype(jnp.float32) * slope_two).astype(jnp.bfloat16)
    act_one, slope_one = gelu_parts(pre_first.astype(jnp.float32))
    act_one = act_one.astype(jnp.bfloat16)
    extended_two = pad_sides(with_halo(grad_two, (("gx", 0),), 1))
    stacked_two = stack_taps(extended_two, -1, z_cells)
    grad_act = back_data(stacked_two, full_second, shape)
    extended_act = pad_sides(with_halo(act_one, (("gx", 0),), 1))
    filt_two = filter_from_inputs(stack_taps(extended_act, 1, z_cells), grad_two, shape)
    owned_two = lax.psum_scatter(filt_two * grad_scale, "gx", scatter_dimension=0, tiled=True)
    grad_one = (grad_act * slope_one).astype(jnp.bfloat16)
    extended_one = pad_sides(with_halo(grad_one, (("gx", 0),), 1))
    stacked_one = stack_taps(extended_one, -1, z_cells)
    grad_in = back_data(stacked_one, full_first, shape).astype(jnp.bfloat16)
    extended_in = pad_sides(with_halo(inputs, (("gx", 0),), 1))
    filt_one = filter_from_inputs(stack_taps(extended_in, 1, z_cells), grad_one, shape)
    owned_one = lax.psum_scatter(filt_one * grad_scale, "gx", scatter_dimension=0, tiled=True)
    return (grad_in, owned_one, owned_two)


MESH = pl.DeviceIdType.MESH
sub = 8


def shift_z(block, shift):
    if shift == 0:
        return block
    cells = block.shape[0]
    row = lax.broadcasted_iota(jnp.int32, block.shape, 0)
    edge = 0 if shift > 0 else cells - 1
    return jnp.where(row == edge, 0.0, pltpu.roll(block, shift % cells, 0))


def kernel(
    n, go_in, xin_in, p1_in, p2_in, f1_in, f2_in, gin, own1, own2,
    go, xin, p1, p2,
    fbuf, wbuf, gext, abuf, sat, gcat, slope, part, s1, r1, s2, r2, s3, r3,
    load, halo_s, halo_r, agz_s, agz_r, agx_s, agx_r, agy_s, agy_r, agc_s, agc_r,
    rs1_s, rs1_r, rs2_s, rs2_r, rs3_s, rs3_r,
):
    xs, ys, zs, ch = go.shape
    units = f1_in.shape[0]
    hi = n // 4
    grad_scale = 1.0 / math.sqrt(xs * n * ys * zs)
    group, me = lax.axis_index("groups"), lax.axis_index("gx")
    core = me % 2
    mid = (me // 2) % 2
    top = me // 4
    partner = me + 1 - 2 * core
    across = me + 2 - 4 * mid
    lead = core == group
    follower = jnp.logical_not(lead)
    upper = top // ((hi + 1) // 2)
    room = top + upper * (hi - 1 - 2 * top)
    place = top + (1 - upper) * (hi - 1 - 2 * top)

    def owner(t, m, c):
        return (t * 2 + m) * 2 + c

    def chunk(t, m, c):
        return pl.ds(owner(t, m, c) * units, units)

    def at_least(value, bound):
        return 1 - 1 // (1 + value // bound)

    def near(k):
        both = at_least(2 * room, k)
        step = both * ((k + 1) // 2) + (1 - both) * (k - room)
        return top + (1 - 2 * upper) * (1 - 2 * both * ((k + 1) % 2)) * step

    def from_far(i):
        return (1 - upper) * (hi - 1 - i) + upper * i

    def far_peer(i):
        return from_far(i + at_least(i + 1, place + 1))

    def remote(src, dst, send, recv, target, plane):
        return pltpu.make_async_remote_copy(
            src_ref=src, dst_ref=dst, send_sem=send, recv_sem=recv,
            device_id=(plane, target), device_id_type=MESH,
        )

    def push(src, dst, send, recv, target, plane=group):
        remote(src, dst, send, recv, target, plane).start()

    def arrive(dst, recv):
        remote(dst, dst, halo_s.at[0, 0], recv, partner, group).wait_recv()

    barrier = pltpu.get_barrier_semaphore()
    peers = [partner, across, lax.rem(me + 1, n), lax.rem(me + n - 1, n)]
    peers += [owner(near(k), mid, core) for k in range(1, hi)]
    for peer in peers:
        pl.semaphore_signal(barrier, inc=1, device_id=(group, peer), device_id_type=MESH)
    pl.semaphore_signal(barrier, inc=1, device_id=(1 - group, me), device_id_type=MESH)

    own_chunk = chunk(top, mid, core)
    loads = [
        pltpu.make_async_copy(src, dst, load.at[i])
        for i, (src, dst) in enumerate(
            (
                (f2_in, fbuf.at[0, own_chunk]), (p2_in, p2), (go_in, go), (p1_in, p1),
                (xin_in, xin), (f1_in, fbuf.at[1, own_chunk]),
            )
        )
    ]
    for copy in loads:
        copy.start()

    for f in range(2):
        for x in range(xs + 2):
            for y in (0, ys + 1):
                gext[f, x, y] = jnp.zeros((zs, ch), jnp.bfloat16)
                gcat[f, x, y] = jnp.zeros((zs, 3 * ch), jnp.bfloat16)

    def gather_spread(f, got, which):
        for k in range(hi - 1, 0, -1):
            push(
                got, got, agz_s.at[f, which, k], agz_r.at[f, which, top],
                owner(near(k), mid, core),
            )

    def gather_own(f):
        mine = fbuf.at[f, own_chunk]
        push(mine, mine, agx_s.at[f], agx_r.at[f], across)

        @pl.when(lead)
        def _():
            gather_spread(f, mine, 0)

        push(mine, mine, agc_s.at[f, 0], agc_r.at[f, mid * hi + top], partner)

    def hand_on(f, got, t, m, k, cross=True):
        if cross:
            push(got, got, agy_s.at[f, k], agy_r.at[f, m * hi + t], me, 1 - group)
        push(got, got, agc_s.at[f, k], agc_r.at[f, m * hi + t], partner)

    def gather_side(f):
        got = fbuf.at[f, chunk(top, 1 - mid, core)]
        arrive(got, agx_r.at[f])

        @pl.when(lead)
        def _():
            gather_spread(f, got, 1)

        hand_on(f, got, top, 1 - mid, hi, False)

    def gather_line(f, side):
        @pl.when(lead)
        def _():
            for k in range(1, hi):
                t = near(k)
                which = 1 - mid if side else mid
                got = fbuf.at[f, chunk(t, which, core)]
                arrive(got, agz_r.at[f, side, t])
                hand_on(f, got, t, which, side * hi + k)

    def gather_follow(f):
        @pl.when(follower)
        def _():
            for half in range(2):
                which = mid + half * (1 - 2 * mid)
                for k in range(1, hi):
                    t = near(k)
                    got = fbuf.at[f, chunk(t, which, core)]
                    arrive(got, agy_r.at[f, which * hi + t])
                    hand_on(f, got, t, which, half * hi + k, False)

    def gather_core(f):
        for m in range(2):
            for t in range(hi):
                arrive(fbuf.at[f, chunk(t, m, 1 - core)], agc_r.at[f, m * hi + t])
        taps = 3 * ch // sub
        for ab in range(9):
            rows = fbuf[f, ab * taps : (ab + 1) * taps].astype(jnp.float32)
            wbuf[f, :, ab * ch : (ab + 1) * ch] = rows.reshape(3 * ch, ch).astype(jnp.bfloat16)

    def halo_copy(h, first, last, low, high):
        to_left = remote(
            first, high, halo_s.at[h, 0], halo_r.at[h, 1], lax.rem(me + n - 1, n), group
        )
        to_right = remote(
            last, low, halo_s.at[h, 1], halo_r.at[h, 0], lax.rem(me + 1, n), group
        )

        @pl.when(me > 0)
        def _():
            to_left.start()

        @pl.when(me < n - 1)
        def _():
            to_right.start()

        return to_left, to_right, low, high, h

    def halo_wait(halo):
        _, _, low, high, h = halo

        @pl.when(me > 0)
        def _():
            arrive(low, halo_r.at[h, 0])

        @pl.when(me == 0)
        def _():
            low[...] = jnp.zeros(low.shape, low.dtype)

        @pl.when(me < n - 1)
        def _():
            arrive(high, halo_r.at[h, 1])

        @pl.when(me == n - 1)
        def _():
            high[...] = jnp.zeros(high.shape, high.dtype)

    def grad_halo(f):
        inner = pl.ds(1, ys)
        return halo_copy(
            f, gext.at[f, 1, inner], gext.at[f, xs, inner],
            gext.at[f, 0, inner], gext.at[f, xs + 1, inner],
        )

    def keep_shifts(f, x, y, value):
        for c in (-1, 0, 1):
            gcat[f, x + 1, y + 1, :, (c + 1) * ch : (c + 2) * ch] = shift_z(value, c).astype(
                jnp.bfloat16
            )

    def keep_grad(f, x, y, value):
        gext[f, x + 1, y + 1] = value.astype(jnp.bfloat16)
        keep_shifts(f, x, y, value)

    def halo_shifts(f):
        for x in (-1, xs):
            for y in range(ys):
                keep_shifts(f, x, y, gext[f, x + 1, y + 1].astype(jnp.float32))

    def turn(s, layer, block):
        for y in range(ys):
            sat[s, layer, :, y * zs : (y + 1) * zs] = block[y].T

    per = ch // sub

    def filter_terms(s, a):
        lhs = jnp.concatenate([sat[s, x] for x in range(xs)], axis=1)
        for b in (-1, 0, 1):
            rhs = gcat[s, pl.ds(2 - a, xs), 1 - b : 1 - b + ys].reshape(xs * ys * zs, 3 * ch)
            out = jnp.dot(lhs, rhs, preferred_element_type=jnp.float32)
            for c in range(3):
                part[s, pl.ds((9 * a + 3 * (b + 1) + c) * per, per)] = out[
                    :, c * ch : (c + 1) * ch
                ].reshape(per, sub, ch)

    def scatter_core(s, i):
        t = from_far(i)
        for m in range(2):
            which = 1 - mid if m == 0 else mid
            s1[s, m, t] = part[s, chunk(t, which, 1 - core)].astype(jnp.bfloat16)
            push(s1.at[s, m, t], r1.at[s, m, t], rs1_s.at[s, m, i], rs1_r.at[s, m, t], partner)

    def terms_out(s):
        for j in range(3):
            filter_terms(s, (1 - upper) * (2 - j) + upper * j)
            for i in range(j * hi // 3, (j + 1) * hi // 3):
                scatter_core(s, i)

    def scatter_mid(s, steps):
        for i in steps:
            t = far_peer(i) if i < hi - 1 else top
            arrive(r1.at[s, 0, t], rs1_r.at[s, 0, t])
            s2[s, t] = (
                part[s, chunk(t, 1 - mid, core)] + r1[s, 0, t].astype(jnp.float32)
            ).astype(jnp.bfloat16)
            push(s2.at[s, t], r2.at[s, t], rs2_s.at[s, i], rs2_r.at[s, t], across)

    def total(s, t):
        arrive(r1.at[s, 1, t], rs1_r.at[s, 1, t])
        arrive(r2.at[s, t], rs2_r.at[s, t])
        return (
            part[s, chunk(t, mid, core)]
            + r1[s, 1, t].astype(jnp.float32)
            + r2[s, t].astype(jnp.float32)
        )

    def scatter_top(s):
        for i in range(hi - 1):
            t = far_peer(i)
            s3[s, t] = total(s, t).astype(jnp.bfloat16)
            push(
                s3.at[s, t], r3.at[s, top], rs3_s.at[s, i], rs3_r.at[s, top],
                owner(t, mid, core),
            )

    def scatter_end(s, out):
        value = total(s, top)
        for i in range(hi - 1, 0, -1):
            t = near(i)
            arrive(r3.at[s, t], rs3_r.at[s, t])
            value = value + r3[s, t].astype(jnp.float32)
        out[...] = value * grad_scale

    def layer_back(f, x):
        lhs = jnp.concatenate(
            [
                gext[f, x + 1 - a, 1 - b : 1 - b + ys].reshape(ys * zs, ch)
                for a in (-1, 0, 1)
                for b in (-1, 0, 1)
            ],
            axis=1,
        )
        wide = lax.dot_general(
            lhs, wbuf[f], (((1,), (1,)), ((), ())), preferred_element_type=jnp.float32
        )
        rows = []
        for y in range(ys):
            block = wide[y * zs : (y + 1) * zs]
            rows.append(
                shift_z(block[:, :ch], -1) + block[:, ch : 2 * ch] + shift_z(block[:, 2 * ch :], 1)
            )
        return rows

    pl.semaphore_wait(barrier, len(peers) + 1)
    loads[0].wait()
    gather_own(0)
    loads[1].wait()
    loads[2].wait()

    @pl.loop(0, xs * ys)
    def _(i):
        x, y = i // ys, i % ys
        _, slope_two = gelu_parts(p2[x, y].astype(jnp.float32))
        keep_grad(0, x, y, go[x, y].astype(jnp.float32) * slope_two)

    halo_two = grad_halo(0)
    loads[3].wait()

    @pl.loop(0, xs * ys)
    def _(i):
        x, y = i // ys, i % ys
        act, slope_one = gelu_parts(p1[x, y].astype(jnp.float32))
        abuf[x, y] = act.astype(jnp.bfloat16)
        slope[x, y] = slope_one

    loads[4].wait()
    for x in range(xs):
        turn(0, x, abuf[x])
        turn(1, x, xin[x])
    loads[5].wait()
    gather_side(0)
    gather_line(0, 0)
    gather_line(0, 1)
    gather_own(1)
    halo_wait(halo_two)
    halo_shifts(0)
    terms_out(0)
    gather_side(1)
    gather_follow(0)
    scatter_mid(0, range(hi // 2))
    gather_core(0)
    for x in range(xs):
        for y, value in enumerate(layer_back(0, x)):
            keep_grad(1, x, y, value * slope[x, y])
    halo_one = grad_halo(1)
    scatter_mid(0, range(hi // 2, hi))
    gather_line(1, 0)
    gather_line(1, 1)
    scatter_top(0)
    halo_wait(halo_one)
    halo_shifts(1)
    terms_out(1)
    scatter_mid(1, range(hi))
    gather_follow(1)
    gather_core(1)
    for x in range(xs):
        for y, value in enumerate(layer_back(1, x)):
            gin[x, y] = value.astype(jnp.bfloat16)
    scatter_top(1)
    scatter_end(0, own2)
    scatter_end(1, own1)

    def left(send):
        remote(
            fbuf.at[0, own_chunk], fbuf.at[0, own_chunk], send, agc_r.at[0, 0], partner, group
        ).wait_send()

    for f in range(2):
        left(agx_s.at[f])
        left(agc_s.at[f, 0])
        for k in range(1, 2 * hi):
            left(agc_s.at[f, k])

        @pl.when(lead)
        def _():
            for k in range(1, hi):
                left(agz_s.at[f, 0, k])
                left(agz_s.at[f, 1, k])
                left(agy_s.at[f, k])
                left(agy_s.at[f, hi + k])

        for i in range(hi):
            for m in range(2):
                left(rs1_s.at[f, m, i])
            left(rs2_s.at[f, i])
        for i in range(hi - 1):
            left(rs3_s.at[f, i])

    for halo in (halo_two, halo_one):

        @pl.when(me > 0)
        def _():
            halo[0].wait_send()

        @pl.when(me < n - 1)
        def _():
            halo[1].wait_send()


def store_kernel(*refs):
    count = (len(refs) - 1) // 2
    copies = [
        pltpu.make_async_copy(refs[i], refs[count + i], refs[-1].at[i]) for i in range(count)
    ]
    for copy in copies:
        copy.start()
    for copy in copies:
        copy.wait()


def store_out(*results):
    return pl.pallas_call(
        store_kernel,
        out_shape=tuple(jax.ShapeDtypeStruct(r.shape, r.dtype) for r in results),
        in_specs=[pl.BlockSpec(memory_space=pltpu.VMEM)] * len(results),
        out_specs=[pl.BlockSpec(memory_space=pl.ANY)] * len(results),
        scratch_shapes=[pltpu.SemaphoreType.DMA((len(results),))],
    )(*(pltpu.with_memory_space_constraint(r, pltpu.VMEM) for r in results))


def fused(grad_out, inputs, pre_first, pre_second, filter_first, filter_second):
    n = lax.axis_size("gx")
    xs, ys, zs, ch = grad_out.shape
    rows = filter_first.shape[0]
    if rows % sub or n % 4 or n < 8 or lax.axis_size("groups") != 2:
        return on_device(grad_out, inputs, pre_first, pre_second, filter_first, filter_second)
    units, hi, bf = rows // sub, n // 4, jnp.bfloat16
    dma = pltpu.SemaphoreType.DMA
    piece = (units, sub, ch)
    block = pltpu.VMEM((xs, ys, zs, ch), bf)
    gin, own1, own2 = pl.pallas_call(
        functools.partial(kernel, n),
        out_shape=(
            pltpu.VMEM(grad_out.shape, bf),
            pltpu.VMEM(piece, jnp.float32),
            pltpu.VMEM(piece, jnp.float32),
        ),
        in_specs=[pl.BlockSpec(memory_space=pl.ANY)] * 6,
        out_specs=[pl.BlockSpec(memory_space=pltpu.VMEM)] * 3,
        scratch_shapes=[
            block, block, block, block,
            pltpu.VMEM((2, n * units, sub, ch), bf),
            pltpu.VMEM((2, 3 * ch, 9 * ch), bf),
            pltpu.VMEM((2, xs + 2, ys + 2, zs, ch), bf),
            block,
            pltpu.VMEM((2, xs, ch, ys * zs), bf),
            pltpu.VMEM((2, xs + 2, ys + 2, zs, 3 * ch), bf),
            pltpu.VMEM((xs, ys, zs, ch), jnp.float32),
            pltpu.VMEM((2, n * units, sub, ch), jnp.float32),
            pltpu.VMEM((2, 2, hi) + piece, bf),
            pltpu.VMEM((2, 2, hi) + piece, bf),
            pltpu.VMEM((2, hi) + piece, bf),
            pltpu.VMEM((2, hi) + piece, bf),
            pltpu.VMEM((2, hi) + piece, bf),
            pltpu.VMEM((2, hi) + piece, bf),
            dma((6,)),
            dma((2, 2)), dma((2, 2)),
            dma((2, 2, hi)), dma((2, 2, hi)),
            dma((2,)), dma((2,)),
            dma((2, 2 * hi)), dma((2, 2 * hi)),
            dma((2, 2 * hi)), dma((2, 2 * hi)),
            dma((2, 2, hi)), dma((2, 2, hi)),
            dma((2, hi)), dma((2, hi)),
            dma((2, hi)), dma((2, hi)),
        ],
        compiler_params=pltpu.CompilerParams(collective_id=0, has_side_effects=True),
    )(
        grad_out, inputs, pre_first, pre_second,
        filter_first.reshape(piece), filter_second.reshape(piece),
    )
    gin, own1, own2 = store_out(gin, own1, own2)
    return gin, own1.reshape(rows, ch), own2.reshape(rows, ch)


def solution(mesh):
    return jax.shard_map(
        fused,
        mesh=mesh,
        in_specs=(
            P(("groups", "gx"), None, None, None),
            P(("groups", "gx"), None, None, None),
            P(("groups", "gx"), None, None, None),
            P(("groups", "gx"), None, None, None),
            P("gx", None),
            P("gx", None),
        ),
        out_specs=(P(("groups", "gx"), None, None, None), P("gx", "groups"), P("gx", "groups")),
        check_vma=False,
    )
```

```python
import functools
import math

import jax
import jax.numpy as jnp
from jax import lax
from jax.experimental import pallas as pl
from jax.experimental.pallas import tpu as pltpu
from jax.sharding import PartitionSpec as P

inv_root_two = 0.7071067811865476
inv_root_twopi = 0.3989422804014327
tap_shifts = ((-1, -1), (-1, 0), (-1, 1), (0, -1), (0, 0), (0, 1), (1, -1), (1, 0), (1, 1))


def with_halo(block, sides, width):
    for axis, dim in sides:
        count = lax.axis_size(axis)
        forward = [(i, i + 1) for i in range(count - 1)]
        backward = [(target, source) for source, target in forward]
        low = lax.ppermute(
            lax.slice_in_dim(block, block.shape[dim] - width, None, axis=dim), axis, forward
        )
        high = lax.ppermute(lax.slice_in_dim(block, 0, width, axis=dim), axis, backward)
        block = jnp.concatenate([low, block, high], axis=dim)
    return block


def gelu_parts(value):
    normal_cdf = 0.5 * (1.0 + lax.erf(value * inv_root_two))
    return (value * normal_cdf, normal_cdf + value * jnp.exp(-0.5 * value * value) * inv_root_twopi)


def pad_sides(extended):
    return jnp.pad(extended, ((0, 0), (1, 1), (1, 1), (0, 0)))


def stack_taps(padded, direction, z_cells):
    return jnp.concatenate(
        [
            padded[:, :, 1 + direction * shift_z : 1 + direction * shift_z + z_cells]
            for shift_z in (-1, 0, 1)
        ],
        axis=3,
    )


def window(stacked, direction, shift_x, shift_y, x_cells, y_cells):
    start_x = 1 + direction * shift_x
    start_y = 1 + direction * shift_y
    return stacked[start_x : start_x + x_cells, start_y : start_y + y_cells]


def back_data(stacked, full_filter, shape):
    x_cells, y_cells, z_cells, channels = shape
    kernel = full_filter.reshape(3, 3, 3, channels, channels)
    running = jnp.zeros((x_cells * y_cells * z_cells, channels), jnp.float32)
    for shift_x, shift_y in tap_shifts:
        tap_matrix = jnp.transpose(kernel[shift_x + 1, shift_y + 1], (0, 2, 1)).reshape(
            3 * channels, channels
        )
        piece = window(stacked, -1, shift_x, shift_y, x_cells, y_cells).reshape(-1, 3 * channels)
        running = running + jnp.dot(piece, tap_matrix, preferred_element_type=jnp.float32)
    return running.reshape(shape)


def filter_from_inputs(stacked, grads, shape):
    x_cells, y_cells, z_cells, channels = shape
    flat_grads = grads.reshape(-1, channels)
    blocks = []
    for shift_x, shift_y in tap_shifts:
        piece = window(stacked, 1, shift_x, shift_y, x_cells, y_cells).reshape(-1, 3 * channels)
        product = lax.dot_general(
            piece, flat_grads, (((0,), (0,)), ((), ())), preferred_element_type=jnp.float32
        )
        blocks.append(product.reshape(3, channels, channels))
    return jnp.stack(blocks).reshape(27 * channels, channels)


def on_device(grad_out, inputs, pre_first, pre_second, filter_first, filter_second):
    shape = grad_out.shape
    x_cells, y_cells, z_cells, channels = shape
    full_first, full_second = (
        lax.all_gather(filter_first, "gx", axis=0, tiled=True),
        lax.all_gather(filter_second, "gx", axis=0, tiled=True),
    )
    grad_scale = 1.0 / math.sqrt(x_cells * lax.axis_size("gx") * y_cells * z_cells)
    unused_value, slope_two = gelu_parts(pre_second.astype(jnp.float32))
    grad_two = (grad_out.astype(jnp.float32) * slope_two).astype(jnp.bfloat16)
    act_one, slope_one = gelu_parts(pre_first.astype(jnp.float32))
    act_one = act_one.astype(jnp.bfloat16)
    extended_two = pad_sides(with_halo(grad_two, (("gx", 0),), 1))
    stacked_two = stack_taps(extended_two, -1, z_cells)
    grad_act = back_data(stacked_two, full_second, shape)
    extended_act = pad_sides(with_halo(act_one, (("gx", 0),), 1))
    filt_two = filter_from_inputs(stack_taps(extended_act, 1, z_cells), grad_two, shape)
    owned_two = lax.psum_scatter(filt_two * grad_scale, "gx", scatter_dimension=0, tiled=True)
    grad_one = (grad_act * slope_one).astype(jnp.bfloat16)
    extended_one = pad_sides(with_halo(grad_one, (("gx", 0),), 1))
    stacked_one = stack_taps(extended_one, -1, z_cells)
    grad_in = back_data(stacked_one, full_first, shape).astype(jnp.bfloat16)
    extended_in = pad_sides(with_halo(inputs, (("gx", 0),), 1))
    filt_one = filter_from_inputs(stack_taps(extended_in, 1, z_cells), grad_one, shape)
    owned_one = lax.psum_scatter(filt_one * grad_scale, "gx", scatter_dimension=0, tiled=True)
    return (grad_in, owned_one, owned_two)


MESH = pl.DeviceIdType.MESH
sub = 8


def shift_z(block, shift):
    if shift == 0:
        return block
    cells = block.shape[0]
    row = lax.broadcasted_iota(jnp.int32, block.shape, 0)
    edge = 0 if shift > 0 else cells - 1
    return jnp.where(row == edge, 0.0, pltpu.roll(block, shift % cells, 0))


def kernel(
    n, go_in, xin_in, p1_in, p2_in, f1_in, f2_in, gin, own1, own2,
    go, xin, p1, p2,
    fbuf, wbuf, gext, abuf, ahalo, sat, turned, gcat, slope, part, s1, r1, s2, r2, s3, r3, rg, s4, r4, rh,
    load, halo_s, halo_r, sent, line_r, relay_r, cross_r, core_r, late_r,
    rs1_r, rs2_r, rs3_r, rsg_r,
):
    xs, ys, zs, ch = go.shape
    units = f1_in.shape[0]
    hi = n // 4
    grad_scale = 1.0 / math.sqrt(xs * n * ys * zs)
    group, me = lax.axis_index("groups"), lax.axis_index("gx")
    core = me % 2
    mid = (me // 2) % 2
    top = me // 4
    partner = me + 1 - 2 * core
    across = me + 2 - 4 * mid
    lead = core == group
    follower = jnp.logical_not(lead)
    upper = top // ((hi + 1) // 2)
    room = top + upper * (hi - 1 - 2 * top)
    place = top + (1 - upper) * (hi - 1 - 2 * top)
    near_side = far = hi // 2
    gate = far - 1 + upper
    outer = top != gate
    gate_slot = (top - gate - 1) % near_side

    def owner(t, m, c):
        return (t * 2 + m) * 2 + c

    def chunk(t, m, c):
        return pl.ds(owner(t, m, c) * units, units)

    def at_least(value, bound):
        return 1 - 1 // (1 + value // bound)

    def near(k):
        both = at_least(2 * room, k)
        step = both * ((k + 1) // 2) + (1 - both) * (k - room)
        return top + (1 - 2 * upper) * (1 - 2 * both * ((k + 1) % 2)) * step

    def from_far(i):
        return (1 - upper) * (hi - 1 - i) + upper * i

    def same_side(k):
        return upper * far + (top - upper * far + k) % near_side

    def far_peer(i):
        return from_far(i + at_least(i + 1, place + 1))

    def remote(src, dst, send, recv, target, plane):
        return pltpu.make_async_remote_copy(
            src_ref=src, dst_ref=dst, send_sem=send, recv_sem=recv,
            device_id=(plane, target), device_id_type=MESH,
        )

    def push(src, dst, count, recv, target, plane=group):
        remote(src, dst, sent.at[count], recv, target, plane).start()

    def arrive(dst, recv):
        remote(dst, dst, sent.at[0], recv, partner, group).wait_recv()

    def pieces(f, count):
        return fbuf.at[f, pl.ds(0, count * units)]

    barrier = pltpu.get_barrier_semaphore()
    peers = [partner, across, lax.rem(me + 1, n), lax.rem(me + n - 1, n)]
    peers += [owner(near(k), mid, core) for k in range(1, hi)]
    for peer in peers:
        pl.semaphore_signal(barrier, inc=1, device_id=(group, peer), device_id_type=MESH)
    pl.semaphore_signal(barrier, inc=1, device_id=(1 - group, me), device_id_type=MESH)

    own_chunk = chunk(top, mid, core)
    loads = [
        pltpu.make_async_copy(src, dst, load.at[i])
        for i, (src, dst) in enumerate(
            (
                (f2_in, fbuf.at[0, own_chunk]), (p2_in, p2), (go_in, go), (p1_in, p1),
                (xin_in, xin), (f1_in, fbuf.at[1, own_chunk]),
            )
        )
    ]
    for copy in loads:
        copy.start()

    for f in range(2):
        for x in range(xs + 2):
            for y in (0, ys + 1):
                gext[f, x, y] = jnp.zeros((zs, ch), jnp.bfloat16)
                gcat[f, x, y] = jnp.zeros((zs, 3 * ch), jnp.bfloat16)

    for x in range(xs + 2):
        for y in (0, ys + 1):
            turned[x, :, y * zs : (y + 1) * zs] = jnp.zeros((ch, zs), jnp.bfloat16)

    def mine(f):
        return fbuf.at[f, own_chunk]

    def to_partner(f, got):
        push(got, got, 3 * f, core_r.at[f], partner)

    def cross(f, got, recv):
        push(got, got, 4 + f, recv, me, 1 - group)
        to_partner(f, got)

    def first_own():
        push(mine(0), mine(0), 0, relay_r.at[top], across)

        @pl.when(lead)
        def _():
            for k in range(hi - 1, 0, -1):
                push(mine(0), mine(0), 4, line_r.at[top], owner(near(k), mid, core))

        to_partner(0, mine(0))

    def first_side():
        got = fbuf.at[0, chunk(top, 1 - mid, core)]
        arrive(got, relay_r.at[top])
        to_partner(0, got)

    def first_line():
        @pl.when(lead)
        def _():
            for k in range(1, hi):
                t = near(k)
                got = fbuf.at[0, chunk(t, mid, core)]
                arrive(got, line_r.at[t])
                push(got, got, 4, relay_r.at[t], across)
                cross(0, got, cross_r.at[mid * hi + t])

    def first_relay():
        @pl.when(lead)
        def _():
            for k in range(1, hi):
                t = near(k)
                got = fbuf.at[0, chunk(t, 1 - mid, core)]
                arrive(got, relay_r.at[t])
                cross(0, got, cross_r.at[(1 - mid) * hi + t])

    def first_follow():
        @pl.when(follower)
        def _():
            for side in range(2):
                which = 1 - mid if side else mid
                for k in range(1, hi):
                    t = near(k)
                    got = fbuf.at[0, chunk(t, which, core)]
                    arrive(got, cross_r.at[which * hi + t])
                    to_partner(0, got)

    def late_own():
        to_partner(1, mine(1))

        @pl.when(lead)
        def _():
            push(mine(1), mine(1), 5, late_r.at[0], across)

    def late_spread():
        @pl.when(lead)
        def _():
            for k in range(hi - 1, 0, -1):
                push(mine(1), mine(1), 5, late_r.at[1], owner(near(k), mid, core))

    def late_line():
        @pl.when(lead)
        def _():
            arrive(pieces(1, hi - 1), late_r.at[1])
            for k in range(1, hi):
                got = fbuf.at[1, chunk(near(k), mid, core)]
                push(got, got, 5, late_r.at[2], across)
                cross(1, got, late_r.at[3])

    def late_relay():
        @pl.when(lead)
        def _():
            arrive(mine(1), late_r.at[0])
            arrive(pieces(1, hi - 1), late_r.at[2])
            for k in range(hi):
                t = near(k) if k else top
                cross(1, fbuf.at[1, chunk(t, 1 - mid, core)], late_r.at[3])

    def late_follow():
        @pl.when(follower)
        def _():
            arrive(pieces(1, 2 * hi - 1), late_r.at[3])
            to_partner(1, fbuf.at[1, chunk(top, 1 - mid, core)])
            for k in range(1, hi):
                for m in range(2):
                    to_partner(1, fbuf.at[1, chunk(near(k), m, core)])

    def gather_core(f):
        arrive(pieces(f, 2 * hi), core_r.at[f])
        taps = 3 * ch // sub
        for ab in range(9):
            rows = fbuf[f, ab * taps : (ab + 1) * taps].astype(jnp.float32)
            wbuf[f, :, ab * ch : (ab + 1) * ch] = rows.reshape(3 * ch, ch).astype(jnp.bfloat16)

    def halo_copy(h, first, last, low, high):
        to_left = remote(
            first, high, halo_s.at[0], halo_r.at[h, 1], lax.rem(me + n - 1, n), group
        )
        to_right = remote(
            last, low, halo_s.at[1], halo_r.at[h, 0], lax.rem(me + 1, n), group
        )

        @pl.when(me > 0)
        def _():
            to_left.start()

        @pl.when(me < n - 1)
        def _():
            to_right.start()

        return low, high, h

    def halo_wait(halo):
        low, high, h = halo

        @pl.when(me > 0)
        def _():
            arrive(low, halo_r.at[h, 0])

        @pl.when(me == 0)
        def _():
            low[...] = jnp.zeros(low.shape, low.dtype)

        @pl.when(me < n - 1)
        def _():
            arrive(high, halo_r.at[h, 1])

        @pl.when(me == n - 1)
        def _():
            high[...] = jnp.zeros(high.shape, high.dtype)

    def grad_halo(f):
        inner = pl.ds(1, ys)
        return halo_copy(
            f, gext.at[f, 1, inner], gext.at[f, xs, inner],
            gext.at[f, 0, inner], gext.at[f, xs + 1, inner],
        )

    def saved_halo(h, block):
        return halo_copy(h, block.at[0], block.at[xs - 1], ahalo.at[0], ahalo.at[1])

    def keep_shifts(f, x, y, value):
        for c in (-1, 0, 1):
            gcat[f, x + 1, y + 1, :, (c + 1) * ch : (c + 2) * ch] = shift_z(value, c).astype(
                jnp.bfloat16
            )

    def keep_grad(f, x, y, value):
        gext[f, x + 1, y + 1] = value.astype(jnp.bfloat16)
        keep_shifts(f, x, y, value)

    def halo_shifts(f):
        for x in (-1, xs):
            for y in range(ys):
                keep_shifts(f, x, y, gext[f, x + 1, y + 1].astype(jnp.float32))

    def turn(layer, block):
        for y in range(ys):
            sat[0, layer, :, y * zs : (y + 1) * zs] = block[y].T

    def turn_input(layer, block):
        for y in range(ys):
            turned[layer, :, (y + 1) * zs : (y + 2) * zs] = block[y].T

    per = ch // sub

    def filter_terms(s, a):
        lhs = jnp.concatenate([sat[s, x] for x in range(xs)], axis=1)
        for b in (-1, 0, 1):
            rhs = gcat[s, pl.ds(2 - a, xs), 1 - b : 1 - b + ys].reshape(xs * ys * zs, 3 * ch)
            out = jnp.dot(lhs, rhs, preferred_element_type=jnp.float32)
            for c in range(3):
                part[s, pl.ds((9 * a + 3 * (b + 1) + c) * per, per)] = out[
                    :, c * ch : (c + 1) * ch
                ].reshape(per, sub, ch)

    def filter_terms_dense(s, a):
        lhs = jnp.concatenate(
            [
                jnp.concatenate(
                    [turned[x + a, :, b * zs : (b + ys) * zs] for x in range(xs)], axis=1
                )
                for b in range(3)
            ],
            axis=0,
        )
        rhs = gcat[s, 1 : xs + 1, 1 : ys + 1].reshape(xs * ys * zs, 3 * ch)
        out = jnp.dot(lhs, rhs, preferred_element_type=jnp.float32)
        for b in range(3):
            for c in range(3):
                part[s, pl.ds((9 * a + 3 * b + c) * per, per)] = out[
                    b * ch : (b + 1) * ch, c * ch : (c + 1) * ch
                ].reshape(per, sub, ch)

    def side_of(j):
        return mid if j else 1 - mid

    def scatter_core(s, i):
        t = from_far(i)
        for j in range(2):
            s1[s, t, j] = part[s, chunk(t, side_of(j), 1 - core)].astype(jnp.bfloat16)
            if s:
                push(s1.at[s, t, j], r1.at[s, t, j], 1 + s, rs1_r.at[s, hi if j else t], partner)
        if not s:
            push(s1.at[s, t], r1.at[s, t], 1 + s, rs1_r.at[s, t], partner)

    def terms_out(s, steps=range(3)):
        for j in steps:
            (filter_terms_dense if s else filter_terms)(s, (1 - upper) * (2 - j) + upper * j)
            for i in range(j * hi // 3, (j + 1) * hi // 3):
                scatter_core(s, i)

    def cell(t, j):
        return chunk(t, side_of(j), core)

    def pair_sum(t):
        arrive(r1.at[0, t], rs1_r.at[0, t])
        return [part[0, cell(t, j)] + r1[0, t, j].astype(jnp.float32) for j in range(2)]

    def line_send(t, values, dst, recv, target):
        for j in range(2):
            s3[t, j] = values[j].astype(jnp.bfloat16)
        push(s3.at[t], dst, 1, recv, owner(target, mid, core))

    def line_out():
        for i in range(far):
            t = from_far(i)
            values = pair_sum(t)

            @pl.when(outer)
            def _():
                line_send(t, values, rg.at[i, gate_slot], rsg_r.at[0, i], gate)

            @pl.when(jnp.logical_not(outer))
            def _():
                for j in range(2):
                    part[0, cell(t, j)] = values[j]

        for k in range(1, near_side):
            t = same_side(k)
            line_send(t, pair_sum(t), r3.at[k - 1], rs3_r.at[0], t)

    def line_gate():
        @pl.when(jnp.logical_not(outer))
        def _():
            for i in range(far):
                t = from_far(i)
                arrive(rg.at[i, pl.ds(0, near_side - 1)], rsg_r.at[0, i])
                values = [part[0, cell(t, j)] for j in range(2)]
                for k in range(near_side - 1):
                    values = [values[j] + rg[i, k, j].astype(jnp.float32) for j in range(2)]
                line_send(t, values, r3.at[near_side - 1], rs3_r.at[0], t)

    def line_end():
        values = pair_sum(top)
        arrive(r3, rs3_r.at[0])
        for k in range(near_side):
            values = [values[j] + r3[k, j].astype(jnp.float32) for j in range(2)]
        part[0, own_chunk] = values[1]
        s2[0, 0] = values[0].astype(jnp.bfloat16)
        push(s2.at[0, 0], r2.at[0, 0], 1, rs2_r.at[0, 0], across)

    def line_store():
        arrive(r2.at[0, 0], rs2_r.at[0, 0])
        own2[...] = (part[0, own_chunk] + r2[0, 0].astype(jnp.float32)) * grad_scale

    def side_out():
        for i in range(hi):
            t = far_peer(i) if i < hi - 1 else top
            arrive(r1.at[1, t, 0], rs1_r.at[1, t])
            s2[1, t] = (part[1, cell(t, 0)] + r1[1, t, 0].astype(jnp.float32)).astype(
                jnp.bfloat16
            )
            push(s2.at[1, t], r2.at[1, t], 2, rs2_r.at[1, t], across)

    def total(t):
        arrive(r2.at[1, t], rs2_r.at[1, t])
        return (
            part[1, cell(t, 1)]
            + r1[1, t, 1].astype(jnp.float32)
            + r2[1, t].astype(jnp.float32)
        )

    def send_last(t, value, dst, recv, target):
        s4[t] = value.astype(jnp.bfloat16)
        push(s4.at[t], dst, 2, recv, owner(target, mid, core))

    def side_line():
        arrive(fbuf.at[0, pl.ds(0, hi * units)], rs1_r.at[1, hi])
        for i in range(far):
            t = from_far(i)
            value = total(t)

            @pl.when(outer)
            def _():
                send_last(t, value, rh.at[i, gate_slot], rsg_r.at[1, i], gate)

            @pl.when(jnp.logical_not(outer))
            def _():
                arrive(rh.at[i, pl.ds(0, near_side - 1)], rsg_r.at[1, i])
                merged = value
                for k in range(near_side - 1):
                    merged = merged + rh[i, k].astype(jnp.float32)
                send_last(t, merged, r4.at[near_side - 1], rs3_r.at[1], t)

        for k in range(1, near_side):
            t = same_side(k)
            send_last(t, total(t), r4.at[k - 1], rs3_r.at[1], t)

    def side_store():
        value = total(top)
        arrive(r4, rs3_r.at[1])
        for k in range(near_side):
            value = value + r4[k].astype(jnp.float32)
        own1[...] = value * grad_scale

    def layer_back(f, x):
        lhs = jnp.concatenate(
            [
                gext[f, x + 1 - a, 1 - b : 1 - b + ys].reshape(ys * zs, ch)
                for a in (-1, 0, 1)
                for b in (-1, 0, 1)
            ],
            axis=1,
        )
        wide = lax.dot_general(
            lhs, wbuf[f], (((1,), (1,)), ((), ())), preferred_element_type=jnp.float32
        )
        rows = []
        for y in range(ys):
            block = wide[y * zs : (y + 1) * zs]
            rows.append(
                shift_z(block[:, :ch], -1) + block[:, ch : 2 * ch] + shift_z(block[:, 2 * ch :], 1)
            )
        return rows

    pl.semaphore_wait(barrier, len(peers) + 1)
    loads[0].wait()
    first_own()
    loads[1].wait()
    loads[2].wait()

    @pl.loop(0, xs * ys)
    def _(i):
        x, y = i // ys, i % ys
        _, slope_two = gelu_parts(p2[x, y].astype(jnp.float32))
        keep_grad(0, x, y, go[x, y].astype(jnp.float32) * slope_two)

    halo_two = grad_halo(0)
    loads[3].wait()

    @pl.loop(0, xs * ys)
    def _(i):
        x, y = i // ys, i % ys
        act, slope_one = gelu_parts(p1[x, y].astype(jnp.float32))
        abuf[x, y] = act.astype(jnp.bfloat16)
        slope[x, y] = slope_one

    loads[4].wait()
    for x in range(xs):
        turn(x, abuf[x])
        turn_input(x + 1, xin[x])
    loads[5].wait()
    first_line()
    late_own()
    late_spread()
    halo_in = saved_halo(2, xin)
    first_side()
    halo_wait(halo_two)
    halo_shifts(0)
    terms_out(0)
    first_relay()
    line_out()
    late_line()
    first_follow()
    gather_core(0)
    for x in range(xs):
        for y, value in enumerate(layer_back(0, x)):
            keep_grad(1, x, y, value * slope[x, y])
    halo_one = grad_halo(1)
    line_gate()
    late_relay()
    halo_wait(halo_in)
    turn_input(0, ahalo[0])
    turn_input(xs + 1, ahalo[1])
    terms_out(1)
    side_out()
    late_follow()
    halo_wait(halo_one)
    gather_core(1)
    for x in range(xs):
        for y, value in enumerate(layer_back(1, x)):
            gin[x, y] = value.astype(jnp.bfloat16)
    line_end()
    side_line()
    line_store()
    side_store()

    def left(count, send):
        remote(pieces(0, count), pieces(0, count), send, core_r.at[0], partner, group).wait_send()

    for i, count in enumerate((2 * hi + 1, 4 * hi - 1, 4 * hi - 1, 2 * hi)):
        left(count, sent.at[i])

    @pl.when(lead)
    def _():
        left(4 * hi - 4, sent.at[4])
        left(4 * hi - 2, sent.at[5])

    layers = gext.at[0, pl.ds(0, 3), pl.ds(1, ys)]

    @pl.when(me > 0)
    def _():
        remote(layers, layers, halo_s.at[0], core_r.at[0], partner, group).wait_send()

    @pl.when(me < n - 1)
    def _():
        remote(layers, layers, halo_s.at[1], core_r.at[0], partner, group).wait_send()


def store_kernel(*refs):
    count = (len(refs) - 1) // 2
    copies = [
        pltpu.make_async_copy(refs[i], refs[count + i], refs[-1].at[i]) for i in range(count)
    ]
    for copy in copies:
        copy.start()
    for copy in copies:
        copy.wait()


def store_out(*results):
    return pl.pallas_call(
        store_kernel,
        out_shape=tuple(jax.ShapeDtypeStruct(r.shape, r.dtype) for r in results),
        in_specs=[pl.BlockSpec(memory_space=pltpu.VMEM)] * len(results),
        out_specs=[pl.BlockSpec(memory_space=pl.ANY)] * len(results),
        scratch_shapes=[pltpu.SemaphoreType.DMA((len(results),))],
    )(*(pltpu.with_memory_space_constraint(r, pltpu.VMEM) for r in results))


def fused(grad_out, inputs, pre_first, pre_second, filter_first, filter_second):
    n = lax.axis_size("gx")
    xs, ys, zs, ch = grad_out.shape
    rows = filter_first.shape[0]
    if rows % sub or n % 8 or n < 16 or lax.axis_size("groups") != 2:
        return on_device(grad_out, inputs, pre_first, pre_second, filter_first, filter_second)
    units, hi, bf = rows // sub, n // 4, jnp.bfloat16
    dma = pltpu.SemaphoreType.DMA
    piece = (units, sub, ch)
    block = pltpu.VMEM((xs, ys, zs, ch), bf)
    gin, own1, own2 = pl.pallas_call(
        functools.partial(kernel, n),
        out_shape=(
            pltpu.VMEM(grad_out.shape, bf),
            pltpu.VMEM(piece, jnp.float32),
            pltpu.VMEM(piece, jnp.float32),
        ),
        in_specs=[pl.BlockSpec(memory_space=pl.ANY)] * 6,
        out_specs=[pl.BlockSpec(memory_space=pltpu.VMEM)] * 3,
        scratch_shapes=[
            block, block, block, block,
            pltpu.VMEM((2, n * units, sub, ch), bf),
            pltpu.VMEM((2, 3 * ch, 9 * ch), bf),
            pltpu.VMEM((2, xs + 2, ys + 2, zs, ch), bf),
            block,
            pltpu.VMEM((2, ys, zs, ch), bf),
            pltpu.VMEM((1, xs, ch, ys * zs), bf),
            pltpu.VMEM((xs + 2, ch, (ys + 2) * zs), bf),
            pltpu.VMEM((2, xs + 2, ys + 2, zs, 3 * ch), bf),
            pltpu.VMEM((xs, ys, zs, ch), jnp.float32),
            pltpu.VMEM((2, n * units, sub, ch), jnp.float32),
            pltpu.VMEM((2, hi, 2) + piece, bf),
            pltpu.VMEM((2, hi, 2) + piece, bf),
            pltpu.VMEM((2, hi) + piece, bf),
            pltpu.VMEM((2, hi) + piece, bf),
            pltpu.VMEM((hi, 2) + piece, bf),
            pltpu.VMEM((hi // 2, 2) + piece, bf),
            pltpu.VMEM((hi // 2, hi // 2, 2) + piece, bf),
            pltpu.VMEM((hi,) + piece, bf),
            pltpu.VMEM((hi // 2,) + piece, bf),
            pltpu.VMEM((hi // 2, hi // 2) + piece, bf),
            dma((6,)), dma((2,)), dma((3, 2)), dma((6,)),
            dma((hi,)), dma((hi,)), dma((2 * hi,)), dma((2,)), dma((4,)),
            dma((2, hi + 1)), dma((2, hi)), dma((2,)), dma((2, hi // 2)),
        ],
        compiler_params=pltpu.CompilerParams(collective_id=0, has_side_effects=True),
    )(
        grad_out, inputs, pre_first, pre_second,
        filter_first.reshape(piece), filter_second.reshape(piece),
    )
    gin, own1, own2 = store_out(gin, own1, own2)
    return gin, own1.reshape(rows, ch), own2.reshape(rows, ch)


def solution(mesh):
    return jax.shard_map(
        fused,
        mesh=mesh,
        in_specs=(
            P(("groups", "gx"), None, None, None),
            P(("groups", "gx"), None, None, None),
            P(("groups", "gx"), None, None, None),
            P(("groups", "gx"), None, None, None),
            P("gx", None),
            P("gx", None),
        ),
        out_specs=(P(("groups", "gx"), None, None, None), P("gx", "groups"), P("gx", "groups")),
        check_vma=False,
    )
```

```python
import functools
import math

import jax
import jax.numpy as jnp
from jax import lax
from jax.experimental import pallas as pl
from jax.experimental.pallas import tpu as pltpu
from jax.sharding import PartitionSpec as P

inv_root_two = 0.7071067811865476
inv_root_twopi = 0.3989422804014327
tap_shifts = ((-1, -1), (-1, 0), (-1, 1), (0, -1), (0, 0), (0, 1), (1, -1), (1, 0), (1, 1))


def with_halo(block, sides, width):
    for axis, dim in sides:
        count = lax.axis_size(axis)
        forward = [(i, i + 1) for i in range(count - 1)]
        backward = [(target, source) for source, target in forward]
        low = lax.ppermute(
            lax.slice_in_dim(block, block.shape[dim] - width, None, axis=dim), axis, forward
        )
        high = lax.ppermute(lax.slice_in_dim(block, 0, width, axis=dim), axis, backward)
        block = jnp.concatenate([low, block, high], axis=dim)
    return block


def gelu_parts(value):
    normal_cdf = 0.5 * (1.0 + lax.erf(value * inv_root_two))
    return (value * normal_cdf, normal_cdf + value * jnp.exp(-0.5 * value * value) * inv_root_twopi)


def pad_sides(extended):
    return jnp.pad(extended, ((0, 0), (1, 1), (1, 1), (0, 0)))


def stack_taps(padded, direction, z_cells):
    return jnp.concatenate(
        [
            padded[:, :, 1 + direction * shift_z : 1 + direction * shift_z + z_cells]
            for shift_z in (-1, 0, 1)
        ],
        axis=3,
    )


def window(stacked, direction, shift_x, shift_y, x_cells, y_cells):
    start_x = 1 + direction * shift_x
    start_y = 1 + direction * shift_y
    return stacked[start_x : start_x + x_cells, start_y : start_y + y_cells]


def back_data(stacked, full_filter, shape):
    x_cells, y_cells, z_cells, channels = shape
    kernel = full_filter.reshape(3, 3, 3, channels, channels)
    running = jnp.zeros((x_cells * y_cells * z_cells, channels), jnp.float32)
    for shift_x, shift_y in tap_shifts:
        tap_matrix = jnp.transpose(kernel[shift_x + 1, shift_y + 1], (0, 2, 1)).reshape(
            3 * channels, channels
        )
        piece = window(stacked, -1, shift_x, shift_y, x_cells, y_cells).reshape(-1, 3 * channels)
        running = running + jnp.dot(piece, tap_matrix, preferred_element_type=jnp.float32)
    return running.reshape(shape)


def filter_from_inputs(stacked, grads, shape):
    x_cells, y_cells, z_cells, channels = shape
    flat_grads = grads.reshape(-1, channels)
    blocks = []
    for shift_x, shift_y in tap_shifts:
        piece = window(stacked, 1, shift_x, shift_y, x_cells, y_cells).reshape(-1, 3 * channels)
        product = lax.dot_general(
            piece, flat_grads, (((0,), (0,)), ((), ())), preferred_element_type=jnp.float32
        )
        blocks.append(product.reshape(3, channels, channels))
    return jnp.stack(blocks).reshape(27 * channels, channels)


def on_device(grad_out, inputs, pre_first, pre_second, filter_first, filter_second):
    shape = grad_out.shape
    x_cells, y_cells, z_cells, channels = shape
    full_first, full_second = (
        lax.all_gather(filter_first, "gx", axis=0, tiled=True),
        lax.all_gather(filter_second, "gx", axis=0, tiled=True),
    )
    grad_scale = 1.0 / math.sqrt(x_cells * lax.axis_size("gx") * y_cells * z_cells)
    unused_value, slope_two = gelu_parts(pre_second.astype(jnp.float32))
    grad_two = (grad_out.astype(jnp.float32) * slope_two).astype(jnp.bfloat16)
    act_one, slope_one = gelu_parts(pre_first.astype(jnp.float32))
    act_one = act_one.astype(jnp.bfloat16)
    extended_two = pad_sides(with_halo(grad_two, (("gx", 0),), 1))
    stacked_two = stack_taps(extended_two, -1, z_cells)
    grad_act = back_data(stacked_two, full_second, shape)
    extended_act = pad_sides(with_halo(act_one, (("gx", 0),), 1))
    filt_two = filter_from_inputs(stack_taps(extended_act, 1, z_cells), grad_two, shape)
    owned_two = lax.psum_scatter(filt_two * grad_scale, "gx", scatter_dimension=0, tiled=True)
    grad_one = (grad_act * slope_one).astype(jnp.bfloat16)
    extended_one = pad_sides(with_halo(grad_one, (("gx", 0),), 1))
    stacked_one = stack_taps(extended_one, -1, z_cells)
    grad_in = back_data(stacked_one, full_first, shape).astype(jnp.bfloat16)
    extended_in = pad_sides(with_halo(inputs, (("gx", 0),), 1))
    filt_one = filter_from_inputs(stack_taps(extended_in, 1, z_cells), grad_one, shape)
    owned_one = lax.psum_scatter(filt_one * grad_scale, "gx", scatter_dimension=0, tiled=True)
    return (grad_in, owned_one, owned_two)


MESH = pl.DeviceIdType.MESH
sub = 8


def shift_z(block, shift):
    if shift == 0:
        return block
    cells = block.shape[0]
    row = lax.broadcasted_iota(jnp.int32, block.shape, 0)
    edge = 0 if shift > 0 else cells - 1
    return jnp.where(row == edge, 0.0, pltpu.roll(block, shift % cells, 0))


def kernel(
    n, go_in, xin_in, p1_in, p2_in, f1_in, f2_in, gin, own1, own2,
    go, xin, p1, p2,
    fbuf, wbuf, gext, abuf, ahalo, sat, turned, gcat, slope, part, s1, r1, s2, r2, s3, r3, rg, s4, r4, rh,
    load, halo_s, halo_r, sent, line_r, relay_r, cross_r, core_r, late_r,
    rs1_r, rs2_r, rs3_r, rsg_r,
):
    xs, ys, zs, ch = go.shape
    units = f1_in.shape[0]
    hi = n // 4
    grad_scale = 1.0 / math.sqrt(xs * n * ys * zs)
    group, me = lax.axis_index("groups"), lax.axis_index("gx")
    core = me % 2
    mid = (me // 2) % 2
    top = me // 4
    partner = me + 1 - 2 * core
    across = me + 2 - 4 * mid
    lead = core == group
    follower = jnp.logical_not(lead)
    upper = top // ((hi + 1) // 2)
    room = top + upper * (hi - 1 - 2 * top)
    place = top + (1 - upper) * (hi - 1 - 2 * top)
    near_side = far = hi // 2
    gate = far - 1 + upper
    outer = top != gate
    gate_slot = (top - gate - 1) % near_side

    def owner(t, m, c):
        return (t * 2 + m) * 2 + c

    def chunk(t, m, c):
        return pl.ds(owner(t, m, c) * units, units)

    def at_least(value, bound):
        return 1 - 1 // (1 + value // bound)

    def near(k):
        both = at_least(2 * room, k)
        step = both * ((k + 1) // 2) + (1 - both) * (k - room)
        return top + (1 - 2 * upper) * (1 - 2 * both * ((k + 1) % 2)) * step

    def from_far(i):
        return (1 - upper) * (hi - 1 - i) + upper * i

    def same_side(k):
        return upper * far + (top - upper * far + k) % near_side

    def far_peer(i):
        return from_far(i + at_least(i + 1, place + 1))

    def remote(src, dst, send, recv, target, plane):
        return pltpu.make_async_remote_copy(
            src_ref=src, dst_ref=dst, send_sem=send, recv_sem=recv,
            device_id=(plane, target), device_id_type=MESH,
        )

    def push(src, dst, count, recv, target, plane=group):
        remote(src, dst, sent.at[count], recv, target, plane).start()

    def arrive(dst, recv):
        remote(dst, dst, sent.at[0], recv, partner, group).wait_recv()

    def pieces(f, count):
        return fbuf.at[f, pl.ds(0, count * units)]

    barrier = pltpu.get_barrier_semaphore()
    peers = [partner, across, lax.rem(me + 1, n), lax.rem(me + n - 1, n)]
    peers += [owner(near(k), mid, core) for k in range(1, hi)]
    for peer in peers:
        pl.semaphore_signal(barrier, inc=1, device_id=(group, peer), device_id_type=MESH)
    pl.semaphore_signal(barrier, inc=1, device_id=(1 - group, me), device_id_type=MESH)

    own_chunk = chunk(top, mid, core)
    loads = [
        pltpu.make_async_copy(src, dst, load.at[i])
        for i, (src, dst) in enumerate(
            (
                (f2_in, fbuf.at[0, own_chunk]), (p2_in, p2), (go_in, go), (p1_in, p1),
                (xin_in, xin), (f1_in, fbuf.at[1, own_chunk]),
            )
        )
    ]
    for copy in loads:
        copy.start()

    for f in range(2):
        for x in range(xs + 2):
            for y in (0, ys + 1):
                gext[f, x, y] = jnp.zeros((zs, ch), jnp.bfloat16)
                gcat[f, x, y] = jnp.zeros((zs, 3 * ch), jnp.bfloat16)

    for x in range(xs + 2):
        for y in (0, ys + 1):
            turned[x, :, y * zs : (y + 1) * zs] = jnp.zeros((ch, zs), jnp.bfloat16)

    def mine(f):
        return fbuf.at[f, own_chunk]

    def to_partner(f, got):
        push(got, got, 3 * f, core_r.at[f], partner)

    def cross(f, got, recv):
        push(got, got, 4 + f, recv, me, 1 - group)
        to_partner(f, got)

    def first_own():
        push(mine(0), mine(0), 0, relay_r.at[top], across)

        @pl.when(lead)
        def _():
            for k in range(hi - 1, 0, -1):
                push(mine(0), mine(0), 4, line_r.at[top], owner(near(k), mid, core))

        to_partner(0, mine(0))

    def first_side():
        got = fbuf.at[0, chunk(top, 1 - mid, core)]
        arrive(got, relay_r.at[top])
        to_partner(0, got)

    def first_line():
        @pl.when(lead)
        def _():
            for k in range(1, hi):
                t = near(k)
                got = fbuf.at[0, chunk(t, mid, core)]
                arrive(got, line_r.at[t])
                push(got, got, 4, relay_r.at[t], across)
                cross(0, got, cross_r.at[mid * hi + t])

    def first_relay():
        @pl.when(lead)
        def _():
            for k in range(1, hi):
                t = near(k)
                got = fbuf.at[0, chunk(t, 1 - mid, core)]
                arrive(got, relay_r.at[t])
                cross(0, got, cross_r.at[(1 - mid) * hi + t])

    def first_follow():
        @pl.when(follower)
        def _():
            for side in range(2):
                which = 1 - mid if side else mid
                for k in range(1, hi):
                    t = near(k)
                    got = fbuf.at[0, chunk(t, which, core)]
                    arrive(got, cross_r.at[which * hi + t])
                    to_partner(0, got)

    def late_own():
        to_partner(1, mine(1))

        @pl.when(lead)
        def _():
            push(mine(1), mine(1), 5, late_r.at[0], across)

    def late_spread():
        @pl.when(lead)
        def _():
            for k in range(hi - 1, 0, -1):
                push(mine(1), mine(1), 5, late_r.at[1], owner(near(k), mid, core))

    def late_line():
        @pl.when(lead)
        def _():
            arrive(pieces(1, hi - 1), late_r.at[1])
            for k in range(1, hi):
                got = fbuf.at[1, chunk(near(k), mid, core)]
                push(got, got, 5, late_r.at[2], across)
                cross(1, got, late_r.at[3])

    def late_relay():
        @pl.when(lead)
        def _():
            arrive(mine(1), late_r.at[0])
            arrive(pieces(1, hi - 1), late_r.at[2])
            for k in range(hi):
                t = near(k) if k else top
                cross(1, fbuf.at[1, chunk(t, 1 - mid, core)], late_r.at[3])

    def late_follow():
        @pl.when(follower)
        def _():
            arrive(pieces(1, 2 * hi - 1), late_r.at[3])
            to_partner(1, fbuf.at[1, chunk(top, 1 - mid, core)])
            for k in range(1, hi):
                for m in range(2):
                    to_partner(1, fbuf.at[1, chunk(near(k), m, core)])

    def gather_core(f):
        arrive(pieces(f, 2 * hi), core_r.at[f])
        taps = 3 * ch // sub
        for ab in range(9):
            rows = fbuf[f, ab * taps : (ab + 1) * taps].astype(jnp.float32)
            wbuf[f, :, ab * ch : (ab + 1) * ch] = rows.reshape(3 * ch, ch).astype(jnp.bfloat16)

    def halo_copy(h, first, last, low, high):
        to_left = remote(
            first, high, halo_s.at[0], halo_r.at[h, 1], lax.rem(me + n - 1, n), group
        )
        to_right = remote(
            last, low, halo_s.at[1], halo_r.at[h, 0], lax.rem(me + 1, n), group
        )

        @pl.when(me > 0)
        def _():
            to_left.start()

        @pl.when(me < n - 1)
        def _():
            to_right.start()

        return low, high, h

    def halo_wait(halo):
        low, high, h = halo

        @pl.when(me > 0)
        def _():
            arrive(low, halo_r.at[h, 0])

        @pl.when(me == 0)
        def _():
            low[...] = jnp.zeros(low.shape, low.dtype)

        @pl.when(me < n - 1)
        def _():
            arrive(high, halo_r.at[h, 1])

        @pl.when(me == n - 1)
        def _():
            high[...] = jnp.zeros(high.shape, high.dtype)

    def grad_halo(f):
        inner = pl.ds(1, ys)
        return halo_copy(
            f, gext.at[f, 1, inner], gext.at[f, xs, inner],
            gext.at[f, 0, inner], gext.at[f, xs + 1, inner],
        )

    def saved_halo(h, block):
        return halo_copy(h, block.at[0], block.at[xs - 1], ahalo.at[0], ahalo.at[1])

    def keep_shifts(f, x, y, value):
        for c in (-1, 0, 1):
            gcat[f, x + 1, y + 1, :, (c + 1) * ch : (c + 2) * ch] = shift_z(value, c).astype(
                jnp.bfloat16
            )

    def keep_grad(f, x, y, value):
        gext[f, x + 1, y + 1] = value.astype(jnp.bfloat16)
        keep_shifts(f, x, y, value)

    def halo_shifts(f):
        for x in (-1, xs):
            for y in range(ys):
                keep_shifts(f, x, y, gext[f, x + 1, y + 1].astype(jnp.float32))

    def turn(layer, block):
        for y in range(ys):
            sat[0, layer, :, y * zs : (y + 1) * zs] = block[y].T

    def turn_input(layer, block):
        for y in range(ys):
            turned[layer, :, (y + 1) * zs : (y + 2) * zs] = block[y].T

    per = ch // sub

    def filter_terms(s, a):
        lhs = jnp.concatenate([sat[s, x] for x in range(xs)], axis=1)
        for b in (-1, 0, 1):
            rhs = gcat[s, pl.ds(2 - a, xs), 1 - b : 1 - b + ys].reshape(xs * ys * zs, 3 * ch)
            out = jnp.dot(lhs, rhs, preferred_element_type=jnp.float32)
            for c in range(3):
                part[s, pl.ds((9 * a + 3 * (b + 1) + c) * per, per)] = out[
                    :, c * ch : (c + 1) * ch
                ].reshape(per, sub, ch)

    def filter_terms_dense(s, a):
        lhs = jnp.concatenate(
            [
                jnp.concatenate(
                    [turned[x + a, :, b * zs : (b + ys) * zs] for x in range(xs)], axis=1
                )
                for b in range(3)
            ],
            axis=0,
        )
        rhs = gcat[s, 1 : xs + 1, 1 : ys + 1].reshape(xs * ys * zs, 3 * ch)
        out = jnp.dot(lhs, rhs, preferred_element_type=jnp.float32)
        for b in range(3):
            for c in range(3):
                part[s, pl.ds((9 * a + 3 * b + c) * per, per)] = out[
                    b * ch : (b + 1) * ch, c * ch : (c + 1) * ch
                ].reshape(per, sub, ch)

    def side_of(j):
        return mid if j else 1 - mid

    def scatter_core(s, i):
        t = from_far(i)
        for j in range(2):
            s1[s, t, j] = part[s, chunk(t, side_of(j), 1 - core)].astype(jnp.bfloat16)
            if s:
                push(s1.at[s, t, j], r1.at[s, t, j], 1 + s, rs1_r.at[s, hi if j else t], partner)
        if not s:
            push(s1.at[s, t], r1.at[s, t], 1 + s, rs1_r.at[s, t], partner)

    def terms_out(s, steps=range(3)):
        for j in steps:
            (filter_terms_dense if s else filter_terms)(s, (1 - upper) * (2 - j) + upper * j)
            for i in range(j * hi // 3, (j + 1) * hi // 3):
                scatter_core(s, i)

    def cell(t, j):
        return chunk(t, side_of(j), core)

    def pair_sum(t):
        arrive(r1.at[0, t], rs1_r.at[0, t])
        return [part[0, cell(t, j)] + r1[0, t, j].astype(jnp.float32) for j in range(2)]

    def line_send(t, values, dst, recv, target):
        for j in range(2):
            s3[t, j] = values[j].astype(jnp.bfloat16)
        push(s3.at[t], dst, 1, recv, owner(target, mid, core))

    def line_out():
        for i in range(far):
            t = from_far(i)
            values = pair_sum(t)

            @pl.when(outer)
            def _():
                line_send(t, values, rg.at[i, gate_slot], rsg_r.at[0, i], gate)

            @pl.when(jnp.logical_not(outer))
            def _():
                for j in range(2):
                    part[0, cell(t, j)] = values[j]

        for k in range(1, near_side):
            t = same_side(k)
            line_send(t, pair_sum(t), r3.at[k - 1], rs3_r.at[0], t)

    def line_gate():
        @pl.when(jnp.logical_not(outer))
        def _():
            for i in range(far):
                t = from_far(i)
                arrive(rg.at[i, pl.ds(0, near_side - 1)], rsg_r.at[0, i])
                values = [part[0, cell(t, j)] for j in range(2)]
                for k in range(near_side - 1):
                    values = [values[j] + rg[i, k, j].astype(jnp.float32) for j in range(2)]
                line_send(t, values, r3.at[near_side - 1], rs3_r.at[0], t)

    def line_end():
        values = pair_sum(top)
        arrive(r3, rs3_r.at[0])
        for k in range(near_side):
            values = [values[j] + r3[k, j].astype(jnp.float32) for j in range(2)]
        part[0, own_chunk] = values[1]
        s2[0, 0] = values[0].astype(jnp.bfloat16)
        push(s2.at[0, 0], r2.at[0, 0], 1, rs2_r.at[0, 0], across)

    def line_store():
        arrive(r2.at[0, 0], rs2_r.at[0, 0])
        own2[...] = (part[0, own_chunk] + r2[0, 0].astype(jnp.float32)) * grad_scale

    def side_out(steps):
        for i in steps:
            t = far_peer(i) if i < hi - 1 else top
            arrive(r1.at[1, t, 0], rs1_r.at[1, t])
            s2[1, t] = (part[1, cell(t, 0)] + r1[1, t, 0].astype(jnp.float32)).astype(
                jnp.bfloat16
            )
            push(s2.at[1, t], r2.at[1, t], 2, rs2_r.at[1, t], across)

    def total(t):
        arrive(r2.at[1, t], rs2_r.at[1, t])
        return (
            part[1, cell(t, 1)]
            + r1[1, t, 1].astype(jnp.float32)
            + r2[1, t].astype(jnp.float32)
        )

    def send_last(t, value, dst, recv, target):
        s4[t] = value.astype(jnp.bfloat16)
        push(s4.at[t], dst, 2, recv, owner(target, mid, core))

    def side_line():
        arrive(fbuf.at[0, pl.ds(0, hi * units)], rs1_r.at[1, hi])
        for i in range(far):
            t = from_far(i)
            value = total(t)

            @pl.when(outer)
            def _():
                send_last(t, value, rh.at[i, gate_slot], rsg_r.at[1, i], gate)

            @pl.when(jnp.logical_not(outer))
            def _():
                arrive(rh.at[i, pl.ds(0, near_side - 1)], rsg_r.at[1, i])
                merged = value
                for k in range(near_side - 1):
                    merged = merged + rh[i, k].astype(jnp.float32)
                send_last(t, merged, r4.at[near_side - 1], rs3_r.at[1], t)

        for k in range(1, near_side):
            t = same_side(k)
            send_last(t, total(t), r4.at[k - 1], rs3_r.at[1], t)

    def side_store():
        value = total(top)
        arrive(r4, rs3_r.at[1])
        for k in range(near_side):
            value = value + r4[k].astype(jnp.float32)
        own1[...] = value * grad_scale

    def layer_back(f, x):
        lhs = jnp.concatenate(
            [
                gext[f, x + 1 - a, 1 - b : 1 - b + ys].reshape(ys * zs, ch)
                for a in (-1, 0, 1)
                for b in (-1, 0, 1)
            ],
            axis=1,
        )
        wide = lax.dot_general(
            lhs, wbuf[f], (((1,), (1,)), ((), ())), preferred_element_type=jnp.float32
        )
        rows = []
        for y in range(ys):
            block = wide[y * zs : (y + 1) * zs]
            rows.append(
                shift_z(block[:, :ch], -1) + block[:, ch : 2 * ch] + shift_z(block[:, 2 * ch :], 1)
            )
        return rows

    pl.semaphore_wait(barrier, len(peers) + 1)
    loads[0].wait()
    first_own()
    loads[1].wait()
    loads[2].wait()

    @pl.loop(0, xs * ys)
    def _(i):
        x, y = i // ys, i % ys
        _, slope_two = gelu_parts(p2[x, y].astype(jnp.float32))
        keep_grad(0, x, y, go[x, y].astype(jnp.float32) * slope_two)

    halo_two = grad_halo(0)
    loads[3].wait()

    @pl.loop(0, xs * ys)
    def _(i):
        x, y = i // ys, i % ys
        act, slope_one = gelu_parts(p1[x, y].astype(jnp.float32))
        abuf[x, y] = act.astype(jnp.bfloat16)
        slope[x, y] = slope_one

    loads[4].wait()
    for x in range(xs):
        turn(x, abuf[x])
        turn_input(x + 1, xin[x])
    loads[5].wait()
    first_line()
    late_own()
    late_spread()
    first_side()
    halo_wait(halo_two)
    halo_shifts(0)
    terms_out(0)
    first_relay()
    halo_in = saved_halo(2, xin)
    line_out()
    late_line()
    first_follow()
    gather_core(0)
    for x in range(xs):
        for y, value in enumerate(layer_back(0, x)):
            keep_grad(1, x, y, value * slope[x, y])
    late_relay()
    halo_wait(halo_in)
    turn_input(0, ahalo[0])
    turn_input(xs + 1, ahalo[1])
    terms_out(1)
    line_gate()
    side_out(range(hi))
    halo_one = grad_halo(1)
    late_follow()
    side_line()
    line_end()
    halo_wait(halo_one)
    gather_core(1)
    for x in range(xs):
        for y, value in enumerate(layer_back(1, x)):
            gin[x, y] = value.astype(jnp.bfloat16)
    line_store()
    side_store()

    def left(count, send):
        remote(pieces(0, count), pieces(0, count), send, core_r.at[0], partner, group).wait_send()

    for i, count in enumerate((2 * hi + 1, 4 * hi - 1, 4 * hi - 1, 2 * hi)):
        left(count, sent.at[i])

    @pl.when(lead)
    def _():
        left(4 * hi - 4, sent.at[4])
        left(4 * hi - 2, sent.at[5])

    layers = gext.at[0, pl.ds(0, 3), pl.ds(1, ys)]

    @pl.when(me > 0)
    def _():
        remote(layers, layers, halo_s.at[0], core_r.at[0], partner, group).wait_send()

    @pl.when(me < n - 1)
    def _():
        remote(layers, layers, halo_s.at[1], core_r.at[0], partner, group).wait_send()


def store_kernel(*refs):
    count = (len(refs) - 1) // 2
    copies = [
        pltpu.make_async_copy(refs[i], refs[count + i], refs[-1].at[i]) for i in range(count)
    ]
    for copy in copies:
        copy.start()
    for copy in copies:
        copy.wait()


def store_out(*results):
    return pl.pallas_call(
        store_kernel,
        out_shape=tuple(jax.ShapeDtypeStruct(r.shape, r.dtype) for r in results),
        in_specs=[pl.BlockSpec(memory_space=pltpu.VMEM)] * len(results),
        out_specs=[pl.BlockSpec(memory_space=pl.ANY)] * len(results),
        scratch_shapes=[pltpu.SemaphoreType.DMA((len(results),))],
    )(*(pltpu.with_memory_space_constraint(r, pltpu.VMEM) for r in results))


def fused(grad_out, inputs, pre_first, pre_second, filter_first, filter_second):
    n = lax.axis_size("gx")
    xs, ys, zs, ch = grad_out.shape
    rows = filter_first.shape[0]
    if rows % sub or n % 8 or n < 16 or lax.axis_size("groups") != 2:
        return on_device(grad_out, inputs, pre_first, pre_second, filter_first, filter_second)
    units, hi, bf = rows // sub, n // 4, jnp.bfloat16
    dma = pltpu.SemaphoreType.DMA
    piece = (units, sub, ch)
    block = pltpu.VMEM((xs, ys, zs, ch), bf)
    gin, own1, own2 = pl.pallas_call(
        functools.partial(kernel, n),
        out_shape=(
            pltpu.VMEM(grad_out.shape, bf),
            pltpu.VMEM(piece, jnp.float32),
            pltpu.VMEM(piece, jnp.float32),
        ),
        in_specs=[pl.BlockSpec(memory_space=pl.ANY)] * 6,
        out_specs=[pl.BlockSpec(memory_space=pltpu.VMEM)] * 3,
        scratch_shapes=[
            block, block, block, block,
            pltpu.VMEM((2, n * units, sub, ch), bf),
            pltpu.VMEM((2, 3 * ch, 9 * ch), bf),
            pltpu.VMEM((2, xs + 2, ys + 2, zs, ch), bf),
            block,
            pltpu.VMEM((2, ys, zs, ch), bf),
            pltpu.VMEM((1, xs, ch, ys * zs), bf),
            pltpu.VMEM((xs + 2, ch, (ys + 2) * zs), bf),
            pltpu.VMEM((2, xs + 2, ys + 2, zs, 3 * ch), bf),
            pltpu.VMEM((xs, ys, zs, ch), jnp.float32),
            pltpu.VMEM((2, n * units, sub, ch), jnp.float32),
            pltpu.VMEM((2, hi, 2) + piece, bf),
            pltpu.VMEM((2, hi, 2) + piece, bf),
            pltpu.VMEM((2, hi) + piece, bf),
            pltpu.VMEM((2, hi) + piece, bf),
            pltpu.VMEM((hi, 2) + piece, bf),
            pltpu.VMEM((hi // 2, 2) + piece, bf),
            pltpu.VMEM((hi // 2, hi // 2, 2) + piece, bf),
            pltpu.VMEM((hi,) + piece, bf),
            pltpu.VMEM((hi // 2,) + piece, bf),
            pltpu.VMEM((hi // 2, hi // 2) + piece, bf),
            dma((6,)), dma((2,)), dma((3, 2)), dma((6,)),
            dma((hi,)), dma((hi,)), dma((2 * hi,)), dma((2,)), dma((4,)),
            dma((2, hi + 1)), dma((2, hi)), dma((2,)), dma((2, hi // 2)),
        ],
        compiler_params=pltpu.CompilerParams(collective_id=0, has_side_effects=True),
    )(
        grad_out, inputs, pre_first, pre_second,
        filter_first.reshape(piece), filter_second.reshape(piece),
    )
    gin, own1, own2 = store_out(gin, own1, own2)
    return gin, own1.reshape(rows, ch), own2.reshape(rows, ch)


def solution(mesh):
    return jax.shard_map(
        fused,
        mesh=mesh,
        in_specs=(
            P(("groups", "gx"), None, None, None),
            P(("groups", "gx"), None, None, None),
            P(("groups", "gx"), None, None, None),
            P(("groups", "gx"), None, None, None),
            P("gx", None),
            P("gx", None),
        ),
        out_specs=(P(("groups", "gx"), None, None, None), P("gx", "groups"), P("gx", "groups")),
        check_vma=False,
    )
```

```python
import functools
import math

import jax
import jax.numpy as jnp
from jax import lax
from jax.experimental import pallas as pl
from jax.experimental.pallas import tpu as pltpu
from jax.sharding import PartitionSpec as P

inv_root_two = 0.7071067811865476
inv_root_twopi = 0.3989422804014327
tap_shifts = ((-1, -1), (-1, 0), (-1, 1), (0, -1), (0, 0), (0, 1), (1, -1), (1, 0), (1, 1))


def with_halo(block, sides, width):
    for axis, dim in sides:
        count = lax.axis_size(axis)
        forward = [(i, i + 1) for i in range(count - 1)]
        backward = [(target, source) for source, target in forward]
        low = lax.ppermute(
            lax.slice_in_dim(block, block.shape[dim] - width, None, axis=dim), axis, forward
        )
        high = lax.ppermute(lax.slice_in_dim(block, 0, width, axis=dim), axis, backward)
        block = jnp.concatenate([low, block, high], axis=dim)
    return block


def gelu_parts(value):
    normal_cdf = 0.5 * (1.0 + lax.erf(value * inv_root_two))
    return (value * normal_cdf, normal_cdf + value * jnp.exp(-0.5 * value * value) * inv_root_twopi)


def pad_sides(extended):
    return jnp.pad(extended, ((0, 0), (1, 1), (1, 1), (0, 0)))


def stack_taps(padded, direction, z_cells):
    return jnp.concatenate(
        [
            padded[:, :, 1 + direction * shift_z : 1 + direction * shift_z + z_cells]
            for shift_z in (-1, 0, 1)
        ],
        axis=3,
    )


def window(stacked, direction, shift_x, shift_y, x_cells, y_cells):
    start_x = 1 + direction * shift_x
    start_y = 1 + direction * shift_y
    return stacked[start_x : start_x + x_cells, start_y : start_y + y_cells]


def back_data(stacked, full_filter, shape):
    x_cells, y_cells, z_cells, channels = shape
    kernel = full_filter.reshape(3, 3, 3, channels, channels)
    running = jnp.zeros((x_cells * y_cells * z_cells, channels), jnp.float32)
    for shift_x, shift_y in tap_shifts:
        tap_matrix = jnp.transpose(kernel[shift_x + 1, shift_y + 1], (0, 2, 1)).reshape(
            3 * channels, channels
        )
        piece = window(stacked, -1, shift_x, shift_y, x_cells, y_cells).reshape(-1, 3 * channels)
        running = running + jnp.dot(piece, tap_matrix, preferred_element_type=jnp.float32)
    return running.reshape(shape)


def filter_from_inputs(stacked, grads, shape):
    x_cells, y_cells, z_cells, channels = shape
    flat_grads = grads.reshape(-1, channels)
    blocks = []
    for shift_x, shift_y in tap_shifts:
        piece = window(stacked, 1, shift_x, shift_y, x_cells, y_cells).reshape(-1, 3 * channels)
        product = lax.dot_general(
            piece, flat_grads, (((0,), (0,)), ((), ())), preferred_element_type=jnp.float32
        )
        blocks.append(product.reshape(3, channels, channels))
    return jnp.stack(blocks).reshape(27 * channels, channels)


def on_device(grad_out, inputs, pre_first, pre_second, filter_first, filter_second):
    shape = grad_out.shape
    x_cells, y_cells, z_cells, channels = shape
    full_first, full_second = (
        lax.all_gather(filter_first, "gx", axis=0, tiled=True),
        lax.all_gather(filter_second, "gx", axis=0, tiled=True),
    )
    grad_scale = 1.0 / math.sqrt(x_cells * lax.axis_size("gx") * y_cells * z_cells)
    unused_value, slope_two = gelu_parts(pre_second.astype(jnp.float32))
    grad_two = (grad_out.astype(jnp.float32) * slope_two).astype(jnp.bfloat16)
    act_one, slope_one = gelu_parts(pre_first.astype(jnp.float32))
    act_one = act_one.astype(jnp.bfloat16)
    extended_two = pad_sides(with_halo(grad_two, (("gx", 0),), 1))
    stacked_two = stack_taps(extended_two, -1, z_cells)
    grad_act = back_data(stacked_two, full_second, shape)
    extended_act = pad_sides(with_halo(act_one, (("gx", 0),), 1))
    filt_two = filter_from_inputs(stack_taps(extended_act, 1, z_cells), grad_two, shape)
    owned_two = lax.psum_scatter(filt_two * grad_scale, "gx", scatter_dimension=0, tiled=True)
    grad_one = (grad_act * slope_one).astype(jnp.bfloat16)
    extended_one = pad_sides(with_halo(grad_one, (("gx", 0),), 1))
    stacked_one = stack_taps(extended_one, -1, z_cells)
    grad_in = back_data(stacked_one, full_first, shape).astype(jnp.bfloat16)
    extended_in = pad_sides(with_halo(inputs, (("gx", 0),), 1))
    filt_one = filter_from_inputs(stack_taps(extended_in, 1, z_cells), grad_one, shape)
    owned_one = lax.psum_scatter(filt_one * grad_scale, "gx", scatter_dimension=0, tiled=True)
    return (grad_in, owned_one, owned_two)


MESH = pl.DeviceIdType.MESH
sub = 8


def shift_z(block, shift):
    if shift == 0:
        return block
    cells = block.shape[0]
    row = lax.broadcasted_iota(jnp.int32, block.shape, 0)
    edge = 0 if shift > 0 else cells - 1
    return jnp.where(row == edge, 0.0, pltpu.roll(block, shift % cells, 0))


def kernel(
    n, go_in, xin_in, p1_in, p2_in, f1_in, f2_in, gin, own1, own2,
    go, xin, p1, p2,
    fbuf, wbuf, gext, abuf, ahalo, sat, turned, gcat, slope, part, s1, r1, s2, r2, s3, r3, rg, s4, r4,
    load, halo_s, halo_r, sent, line_r, relay_r, cross_r, core_r, late_r,
    rs1_r, rs2_r, rs3_r, rsg_r,
):
    xs, ys, zs, ch = go.shape
    units = f1_in.shape[0]
    hi = n // 4
    grad_scale = 1.0 / math.sqrt(xs * n * ys * zs)
    group, me = lax.axis_index("groups"), lax.axis_index("gx")
    core = me % 2
    mid = (me // 2) % 2
    top = me // 4
    partner = me + 1 - 2 * core
    across = me + 2 - 4 * mid
    lead = core == group
    follower = jnp.logical_not(lead)
    upper = top // ((hi + 1) // 2)
    room = top + upper * (hi - 1 - 2 * top)
    place = top + (1 - upper) * (hi - 1 - 2 * top)
    near_side = far = hi // 2
    gate = far - 1 + upper
    outer = top != gate
    gate_slot = (top - gate - 1) % near_side

    def owner(t, m, c):
        return (t * 2 + m) * 2 + c

    def chunk(t, m, c):
        return pl.ds(owner(t, m, c) * units, units)

    def at_least(value, bound):
        return 1 - 1 // (1 + value // bound)

    def near(k):
        both = at_least(2 * room, k)
        step = both * ((k + 1) // 2) + (1 - both) * (k - room)
        return top + (1 - 2 * upper) * (1 - 2 * both * ((k + 1) % 2)) * step

    def from_far(i):
        return (1 - upper) * (hi - 1 - i) + upper * i

    def same_side(k):
        return upper * far + (top - upper * far + k) % near_side

    def low_peer(i):
        return i + at_least(i + 1, top + 1)

    def remote(src, dst, send, recv, target, plane):
        return pltpu.make_async_remote_copy(
            src_ref=src, dst_ref=dst, send_sem=send, recv_sem=recv,
            device_id=(plane, target), device_id_type=MESH,
        )

    def push(src, dst, count, recv, target, plane=group):
        remote(src, dst, sent.at[count], recv, target, plane).start()

    def arrive(dst, recv):
        remote(dst, dst, sent.at[0], recv, partner, group).wait_recv()

    def pieces(f, count):
        return fbuf.at[f, pl.ds(0, count * units)]

    barrier = pltpu.get_barrier_semaphore()
    peers = [partner, across, lax.rem(me + 1, n), lax.rem(me + n - 1, n)]
    peers += [owner(near(k), mid, core) for k in range(1, hi)]
    for peer in peers:
        pl.semaphore_signal(barrier, inc=1, device_id=(group, peer), device_id_type=MESH)
    pl.semaphore_signal(barrier, inc=1, device_id=(1 - group, me), device_id_type=MESH)

    own_chunk = chunk(top, mid, core)
    loads = [
        pltpu.make_async_copy(src, dst, load.at[i])
        for i, (src, dst) in enumerate(
            (
                (f2_in, fbuf.at[0, own_chunk]), (p2_in, p2), (go_in, go), (p1_in, p1),
                (xin_in, xin), (f1_in, fbuf.at[1, own_chunk]),
            )
        )
    ]
    for copy in loads:
        copy.start()

    for f in range(2):
        for x in range(xs + 2):
            for y in (0, ys + 1):
                gext[f, x, y] = jnp.zeros((zs, ch), jnp.bfloat16)
                gcat[f, x, y] = jnp.zeros((zs, 3 * ch), jnp.bfloat16)

    for x in range(xs + 2):
        for y in (0, ys + 1):
            turned[x, :, y * zs : (y + 1) * zs] = jnp.zeros((ch, zs), jnp.bfloat16)

    def mine(f):
        return fbuf.at[f, own_chunk]

    def to_partner(f, got):
        push(got, got, 3 * f, core_r.at[f], partner)

    def cross(f, got, recv):
        push(got, got, 4 + f, recv, me, 1 - group)
        to_partner(f, got)

    def first_own():
        push(mine(0), mine(0), 0, relay_r.at[top], across)

        @pl.when(lead)
        def _():
            for k in range(hi - 1, 0, -1):
                push(mine(0), mine(0), 4, line_r.at[top], owner(near(k), mid, core))

        to_partner(0, mine(0))

    def first_side():
        got = fbuf.at[0, chunk(top, 1 - mid, core)]
        arrive(got, relay_r.at[top])
        to_partner(0, got)

    def first_line():
        @pl.when(lead)
        def _():
            for k in range(1, hi):
                t = near(k)
                got = fbuf.at[0, chunk(t, mid, core)]
                arrive(got, line_r.at[t])
                push(got, got, 4, relay_r.at[t], across)
                cross(0, got, cross_r.at[mid * hi + t])

    def first_relay():
        @pl.when(lead)
        def _():
            for k in range(1, hi):
                t = near(k)
                got = fbuf.at[0, chunk(t, 1 - mid, core)]
                arrive(got, relay_r.at[t])
                cross(0, got, cross_r.at[(1 - mid) * hi + t])

    def first_follow():
        @pl.when(follower)
        def _():
            for side in range(2):
                which = 1 - mid if side else mid
                for k in range(1, hi):
                    t = near(k)
                    got = fbuf.at[0, chunk(t, which, core)]
                    arrive(got, cross_r.at[which * hi + t])
                    to_partner(0, got)

    def late_own():
        to_partner(1, mine(1))

        @pl.when(lead)
        def _():
            push(mine(1), mine(1), 5, late_r.at[0], across)

    def late_spread():
        @pl.when(lead)
        def _():
            for k in range(hi - 1, 0, -1):
                push(mine(1), mine(1), 5, late_r.at[1], owner(near(k), mid, core))

    def late_line():
        @pl.when(lead)
        def _():
            arrive(pieces(1, hi - 1), late_r.at[1])
            for k in range(1, hi):
                got = fbuf.at[1, chunk(near(k), mid, core)]
                push(got, got, 5, late_r.at[2], across)
                cross(1, got, late_r.at[3])

    def late_relay():
        @pl.when(lead)
        def _():
            arrive(mine(1), late_r.at[0])
            arrive(pieces(1, hi - 1), late_r.at[2])
            for k in range(hi):
                t = near(k) if k else top
                cross(1, fbuf.at[1, chunk(t, 1 - mid, core)], late_r.at[3])

    def late_follow():
        @pl.when(follower)
        def _():
            arrive(pieces(1, 2 * hi - 1), late_r.at[3])
            to_partner(1, fbuf.at[1, chunk(top, 1 - mid, core)])
            for k in range(1, hi):
                for m in range(2):
                    to_partner(1, fbuf.at[1, chunk(near(k), m, core)])

    def gather_core(f):
        arrive(pieces(f, 2 * hi), core_r.at[f])
        taps = 3 * ch // sub
        for ab in range(9):
            rows = fbuf[f, ab * taps : (ab + 1) * taps].astype(jnp.float32)
            wbuf[f, :, ab * ch : (ab + 1) * ch] = rows.reshape(3 * ch, ch).astype(jnp.bfloat16)

    def halo_copy(h, first, last, low, high):
        to_left = remote(
            first, high, halo_s.at[0], halo_r.at[h, 1], lax.rem(me + n - 1, n), group
        )
        to_right = remote(
            last, low, halo_s.at[1], halo_r.at[h, 0], lax.rem(me + 1, n), group
        )

        @pl.when(me > 0)
        def _():
            to_left.start()

        @pl.when(me < n - 1)
        def _():
            to_right.start()

        return low, high, h

    def halo_wait(halo):
        low, high, h = halo

        @pl.when(me > 0)
        def _():
            arrive(low, halo_r.at[h, 0])

        @pl.when(me == 0)
        def _():
            low[...] = jnp.zeros(low.shape, low.dtype)

        @pl.when(me < n - 1)
        def _():
            arrive(high, halo_r.at[h, 1])

        @pl.when(me == n - 1)
        def _():
            high[...] = jnp.zeros(high.shape, high.dtype)

    def grad_halo(f):
        inner = pl.ds(1, ys)
        return halo_copy(
            f, gext.at[f, 1, inner], gext.at[f, xs, inner],
            gext.at[f, 0, inner], gext.at[f, xs + 1, inner],
        )

    def saved_halo(h, block):
        return halo_copy(h, block.at[0], block.at[xs - 1], ahalo.at[0], ahalo.at[1])

    def keep_shifts(f, x, y, value):
        for c in (-1, 0, 1):
            gcat[f, x + 1, y + 1, :, (c + 1) * ch : (c + 2) * ch] = shift_z(value, c).astype(
                jnp.bfloat16
            )

    def keep_grad(f, x, y, value):
        gext[f, x + 1, y + 1] = value.astype(jnp.bfloat16)
        keep_shifts(f, x, y, value)

    def halo_shifts(f):
        for x in (-1, xs):
            for y in range(ys):
                keep_shifts(f, x, y, gext[f, x + 1, y + 1].astype(jnp.float32))

    def turn(layer, block):
        for y in range(ys):
            sat[0, layer, :, y * zs : (y + 1) * zs] = block[y].T

    def turn_input(layer, block):
        for y in range(ys):
            turned[layer, :, (y + 1) * zs : (y + 2) * zs] = block[y].T

    per = ch // sub

    def filter_terms(s, a):
        lhs = jnp.concatenate([sat[s, x] for x in range(xs)], axis=1)
        for b in (-1, 0, 1):
            rhs = gcat[s, pl.ds(2 - a, xs), 1 - b : 1 - b + ys].reshape(xs * ys * zs, 3 * ch)
            out = jnp.dot(lhs, rhs, preferred_element_type=jnp.float32)
            for c in range(3):
                part[s, pl.ds((9 * a + 3 * (b + 1) + c) * per, per)] = out[
                    :, c * ch : (c + 1) * ch
                ].reshape(per, sub, ch)

    def filter_terms_dense(s, a):
        lhs = jnp.concatenate(
            [
                jnp.concatenate(
                    [turned[x + a, :, b * zs : (b + ys) * zs] for x in range(xs)], axis=1
                )
                for b in range(3)
            ],
            axis=0,
        )
        rhs = gcat[s, 1 : xs + 1, 1 : ys + 1].reshape(xs * ys * zs, 3 * ch)
        out = jnp.dot(lhs, rhs, preferred_element_type=jnp.float32)
        for b in range(3):
            for c in range(3):
                part[s, pl.ds((9 * a + 3 * b + c) * per, per)] = out[
                    b * ch : (b + 1) * ch, c * ch : (c + 1) * ch
                ].reshape(per, sub, ch)

    def side_of(j):
        return mid if j else 1 - mid

    def scatter_core(s, i):
        t = i if s else from_far(i)
        for j in range(2):
            s1[s, t, j] = part[s, chunk(t, side_of(j), 1 - core)].astype(jnp.bfloat16)
            if s:
                push(s1.at[s, t, j], r1.at[s, t, j], 1 + s, rs1_r.at[s, hi if j else t], partner)
        if not s:
            push(s1.at[s, t], r1.at[s, t], 1 + s, rs1_r.at[s, t], partner)

    def terms_out(s, steps=range(3)):
        for j in steps:
            if s:
                filter_terms_dense(s, j)
            else:
                filter_terms(s, (1 - upper) * (2 - j) + upper * j)
            for i in range(j * hi // 3, (j + 1) * hi // 3):
                scatter_core(s, i)

    def cell(t, j):
        return chunk(t, side_of(j), core)

    def pair_sum(t):
        arrive(r1.at[0, t], rs1_r.at[0, t])
        return [part[0, cell(t, j)] + r1[0, t, j].astype(jnp.float32) for j in range(2)]

    def line_send(t, values, dst, recv, target):
        for j in range(2):
            s3[t, j] = values[j].astype(jnp.bfloat16)
        push(s3.at[t], dst, 1, recv, owner(target, mid, core))

    def line_out():
        for i in range(far):
            t = from_far(i)
            values = pair_sum(t)

            @pl.when(outer)
            def _():
                line_send(t, values, rg.at[i, gate_slot], rsg_r.at[0, i], gate)

            @pl.when(jnp.logical_not(outer))
            def _():
                for j in range(2):
                    part[0, cell(t, j)] = values[j]

        for k in range(1, near_side):
            t = same_side(k)
            line_send(t, pair_sum(t), r3.at[k - 1], rs3_r.at[0], t)

    def line_gate(steps):
        @pl.when(jnp.logical_not(outer))
        def _():
            for i in steps:
                t = from_far(i)
                arrive(rg.at[i, pl.ds(0, near_side - 1)], rsg_r.at[0, i])
                values = [part[0, cell(t, j)] for j in range(2)]
                for k in range(near_side - 1):
                    values = [values[j] + rg[i, k, j].astype(jnp.float32) for j in range(2)]
                line_send(t, values, r3.at[near_side - 1], rs3_r.at[0], t)

    def line_end():
        values = pair_sum(top)
        arrive(r3, rs3_r.at[0])
        for k in range(near_side):
            values = [values[j] + r3[k, j].astype(jnp.float32) for j in range(2)]
        part[0, own_chunk] = values[1]
        s2[0, 0] = values[0].astype(jnp.bfloat16)
        push(s2.at[0, 0], r2.at[0, 0], 1, rs2_r.at[0, 0], across)

    def line_store():
        arrive(r2.at[0, 0], rs2_r.at[0, 0])
        own2[...] = (part[0, own_chunk] + r2[0, 0].astype(jnp.float32)) * grad_scale

    def side_out(steps):
        for i in steps:
            t = low_peer(i) if i < hi - 1 else top
            arrive(r1.at[1, t, 0], rs1_r.at[1, t])
            s2[1, t] = (part[1, cell(t, 0)] + r1[1, t, 0].astype(jnp.float32)).astype(
                jnp.bfloat16
            )
            push(s2.at[1, t], r2.at[1, t], 2, rs2_r.at[1, t], across)

    def total(t):
        arrive(r2.at[1, t], rs2_r.at[1, t])
        return (
            part[1, cell(t, 1)]
            + r1[1, t, 1].astype(jnp.float32)
            + r2[1, t].astype(jnp.float32)
        )

    def send_last(t, value, dst, recv, target):
        s4[t] = value.astype(jnp.bfloat16)
        push(s4.at[t], dst, 2, recv, owner(target, mid, core))

    def side_line(steps):
        if 0 in steps:
            arrive(fbuf.at[0, pl.ds(0, hi * units)], rs1_r.at[1, hi])
        for i in steps:
            t = low_peer(i)
            send_last(t, total(t), r4.at[top - at_least(top, t + 1)], rs3_r.at[1], t)

    def side_store():
        value = total(top)
        arrive(r4, rs3_r.at[1])
        for k in range(hi - 1):
            value = value + r4[k].astype(jnp.float32)
        own1[...] = value * grad_scale

    def layer_back(f, x):
        lhs = jnp.concatenate(
            [
                gext[f, x + 1 - a, 1 - b : 1 - b + ys].reshape(ys * zs, ch)
                for a in (-1, 0, 1)
                for b in (-1, 0, 1)
            ],
            axis=1,
        )
        wide = lax.dot_general(
            lhs, wbuf[f], (((1,), (1,)), ((), ())), preferred_element_type=jnp.float32
        )
        rows = []
        for y in range(ys):
            block = wide[y * zs : (y + 1) * zs]
            rows.append(
                shift_z(block[:, :ch], -1) + block[:, ch : 2 * ch] + shift_z(block[:, 2 * ch :], 1)
            )
        return rows

    pl.semaphore_wait(barrier, len(peers) + 1)
    loads[0].wait()
    first_own()
    loads[1].wait()
    loads[2].wait()

    @pl.loop(0, xs * ys)
    def _(i):
        x, y = i // ys, i % ys
        _, slope_two = gelu_parts(p2[x, y].astype(jnp.float32))
        keep_grad(0, x, y, go[x, y].astype(jnp.float32) * slope_two)

    halo_two = grad_halo(0)
    loads[3].wait()

    @pl.loop(0, xs * ys)
    def _(i):
        x, y = i // ys, i % ys
        act, slope_one = gelu_parts(p1[x, y].astype(jnp.float32))
        abuf[x, y] = act.astype(jnp.bfloat16)
        slope[x, y] = slope_one

    loads[4].wait()
    for x in range(xs):
        turn(x, abuf[x])
        turn_input(x + 1, xin[x])
    loads[5].wait()
    first_line()
    late_own()
    late_spread()
    first_side()
    halo_wait(halo_two)
    halo_shifts(0)
    terms_out(0)
    first_relay()
    halo_in = saved_halo(2, xin)
    line_out()
    late_line()
    first_follow()
    gather_core(0)
    for x in range(xs):
        for y, value in enumerate(layer_back(0, x)):
            keep_grad(1, x, y, value * slope[x, y])
    halo_one = grad_halo(1)
    line_gate((0,))
    late_relay()
    halo_wait(halo_in)
    turn_input(0, ahalo[0])
    turn_input(xs + 1, ahalo[1])
    terms_out(1)
    line_gate(range(1, far))
    side_out(range(hi))
    late_follow()
    side_line(range(1))
    halo_wait(halo_one)
    gather_core(1)
    for x in range(xs):
        for y, value in enumerate(layer_back(1, x)):
            gin[x, y] = value.astype(jnp.bfloat16)
    side_line(range(1, hi - 2))
    line_end()
    side_line(range(hi - 2, hi - 1))
    line_store()
    side_store()

    def left(count, send):
        remote(pieces(0, count), pieces(0, count), send, core_r.at[0], partner, group).wait_send()

    for i, count in enumerate((2 * hi + 1, 4 * hi - 1, 4 * hi - 1, 2 * hi)):
        left(count, sent.at[i])

    @pl.when(lead)
    def _():
        left(4 * hi - 4, sent.at[4])
        left(4 * hi - 2, sent.at[5])

    layers = gext.at[0, pl.ds(0, 3), pl.ds(1, ys)]

    @pl.when(me > 0)
    def _():
        remote(layers, layers, halo_s.at[0], core_r.at[0], partner, group).wait_send()

    @pl.when(me < n - 1)
    def _():
        remote(layers, layers, halo_s.at[1], core_r.at[0], partner, group).wait_send()


def store_kernel(*refs):
    count = (len(refs) - 1) // 2
    copies = [
        pltpu.make_async_copy(refs[i], refs[count + i], refs[-1].at[i]) for i in range(count)
    ]
    for copy in copies:
        copy.start()
    for copy in copies:
        copy.wait()


def store_out(*results):
    return pl.pallas_call(
        store_kernel,
        out_shape=tuple(jax.ShapeDtypeStruct(r.shape, r.dtype) for r in results),
        in_specs=[pl.BlockSpec(memory_space=pltpu.VMEM)] * len(results),
        out_specs=[pl.BlockSpec(memory_space=pl.ANY)] * len(results),
        scratch_shapes=[pltpu.SemaphoreType.DMA((len(results),))],
    )(*(pltpu.with_memory_space_constraint(r, pltpu.VMEM) for r in results))


def fused(grad_out, inputs, pre_first, pre_second, filter_first, filter_second):
    n = lax.axis_size("gx")
    xs, ys, zs, ch = grad_out.shape
    rows = filter_first.shape[0]
    if rows % sub or n % 8 or n < 16 or lax.axis_size("groups") != 2:
        return on_device(grad_out, inputs, pre_first, pre_second, filter_first, filter_second)
    units, hi, bf = rows // sub, n // 4, jnp.bfloat16
    dma = pltpu.SemaphoreType.DMA
    piece = (units, sub, ch)
    block = pltpu.VMEM((xs, ys, zs, ch), bf)
    gin, own1, own2 = pl.pallas_call(
        functools.partial(kernel, n),
        out_shape=(
            pltpu.VMEM(grad_out.shape, bf),
            pltpu.VMEM(piece, jnp.float32),
            pltpu.VMEM(piece, jnp.float32),
        ),
        in_specs=[pl.BlockSpec(memory_space=pl.ANY)] * 6,
        out_specs=[pl.BlockSpec(memory_space=pltpu.VMEM)] * 3,
        scratch_shapes=[
            block, block, block, block,
            pltpu.VMEM((2, n * units, sub, ch), bf),
            pltpu.VMEM((2, 3 * ch, 9 * ch), bf),
            pltpu.VMEM((2, xs + 2, ys + 2, zs, ch), bf),
            block,
            pltpu.VMEM((2, ys, zs, ch), bf),
            pltpu.VMEM((1, xs, ch, ys * zs), bf),
            pltpu.VMEM((xs + 2, ch, (ys + 2) * zs), bf),
            pltpu.VMEM((2, xs + 2, ys + 2, zs, 3 * ch), bf),
            pltpu.VMEM((xs, ys, zs, ch), jnp.float32),
            pltpu.VMEM((2, n * units, sub, ch), jnp.float32),
            pltpu.VMEM((2, hi, 2) + piece, bf),
            pltpu.VMEM((2, hi, 2) + piece, bf),
            pltpu.VMEM((2, hi) + piece, bf),
            pltpu.VMEM((2, hi) + piece, bf),
            pltpu.VMEM((hi, 2) + piece, bf),
            pltpu.VMEM((hi // 2, 2) + piece, bf),
            pltpu.VMEM((hi // 2, hi // 2, 2) + piece, bf),
            pltpu.VMEM((hi,) + piece, bf),
            pltpu.VMEM((hi - 1,) + piece, bf),
            dma((6,)), dma((2,)), dma((3, 2)), dma((6,)),
            dma((hi,)), dma((hi,)), dma((2 * hi,)), dma((2,)), dma((4,)),
            dma((2, hi + 1)), dma((2, hi)), dma((2,)), dma((1, hi // 2)),
        ],
        compiler_params=pltpu.CompilerParams(collective_id=0, has_side_effects=True),
    )(
        grad_out, inputs, pre_first, pre_second,
        filter_first.reshape(piece), filter_second.reshape(piece),
    )
    gin, own1, own2 = store_out(gin, own1, own2)
    return gin, own1.reshape(rows, ch), own2.reshape(rows, ch)


def solution(mesh):
    return jax.shard_map(
        fused,
        mesh=mesh,
        in_specs=(
            P(("groups", "gx"), None, None, None),
            P(("groups", "gx"), None, None, None),
            P(("groups", "gx"), None, None, None),
            P(("groups", "gx"), None, None, None),
            P("gx", None),
            P("gx", None),
        ),
        out_specs=(P(("groups", "gx"), None, None, None), P("gx", "groups"), P("gx", "groups")),
        check_vma=False,
    )
```

```python
import functools
import math

import jax
import jax.numpy as jnp
from jax import lax
from jax.experimental import pallas as pl
from jax.experimental.pallas import tpu as pltpu
from jax.sharding import PartitionSpec as P

inv_root_two = 0.7071067811865476
inv_root_twopi = 0.3989422804014327
tap_shifts = ((-1, -1), (-1, 0), (-1, 1), (0, -1), (0, 0), (0, 1), (1, -1), (1, 0), (1, 1))


def with_halo(block, sides, width):
    for axis, dim in sides:
        count = lax.axis_size(axis)
        forward = [(i, i + 1) for i in range(count - 1)]
        backward = [(target, source) for source, target in forward]
        low = lax.ppermute(
            lax.slice_in_dim(block, block.shape[dim] - width, None, axis=dim), axis, forward
        )
        high = lax.ppermute(lax.slice_in_dim(block, 0, width, axis=dim), axis, backward)
        block = jnp.concatenate([low, block, high], axis=dim)
    return block


def gelu_parts(value):
    normal_cdf = 0.5 * (1.0 + lax.erf(value * inv_root_two))
    return (value * normal_cdf, normal_cdf + value * jnp.exp(-0.5 * value * value) * inv_root_twopi)


def pad_sides(extended):
    return jnp.pad(extended, ((0, 0), (1, 1), (1, 1), (0, 0)))


def stack_taps(padded, direction, z_cells):
    return jnp.concatenate(
        [
            padded[:, :, 1 + direction * shift_z : 1 + direction * shift_z + z_cells]
            for shift_z in (-1, 0, 1)
        ],
        axis=3,
    )


def window(stacked, direction, shift_x, shift_y, x_cells, y_cells):
    start_x = 1 + direction * shift_x
    start_y = 1 + direction * shift_y
    return stacked[start_x : start_x + x_cells, start_y : start_y + y_cells]


def back_data(stacked, full_filter, shape):
    x_cells, y_cells, z_cells, channels = shape
    kernel = full_filter.reshape(3, 3, 3, channels, channels)
    running = jnp.zeros((x_cells * y_cells * z_cells, channels), jnp.float32)
    for shift_x, shift_y in tap_shifts:
        tap_matrix = jnp.transpose(kernel[shift_x + 1, shift_y + 1], (0, 2, 1)).reshape(
            3 * channels, channels
        )
        piece = window(stacked, -1, shift_x, shift_y, x_cells, y_cells).reshape(-1, 3 * channels)
        running = running + jnp.dot(piece, tap_matrix, preferred_element_type=jnp.float32)
    return running.reshape(shape)


def filter_from_inputs(stacked, grads, shape):
    x_cells, y_cells, z_cells, channels = shape
    flat_grads = grads.reshape(-1, channels)
    blocks = []
    for shift_x, shift_y in tap_shifts:
        piece = window(stacked, 1, shift_x, shift_y, x_cells, y_cells).reshape(-1, 3 * channels)
        product = lax.dot_general(
            piece, flat_grads, (((0,), (0,)), ((), ())), preferred_element_type=jnp.float32
        )
        blocks.append(product.reshape(3, channels, channels))
    return jnp.stack(blocks).reshape(27 * channels, channels)


def on_device(grad_out, inputs, pre_first, pre_second, filter_first, filter_second):
    shape = grad_out.shape
    x_cells, y_cells, z_cells, channels = shape
    full_first, full_second = (
        lax.all_gather(filter_first, "gx", axis=0, tiled=True),
        lax.all_gather(filter_second, "gx", axis=0, tiled=True),
    )
    grad_scale = 1.0 / math.sqrt(x_cells * lax.axis_size("gx") * y_cells * z_cells)
    unused_value, slope_two = gelu_parts(pre_second.astype(jnp.float32))
    grad_two = (grad_out.astype(jnp.float32) * slope_two).astype(jnp.bfloat16)
    act_one, slope_one = gelu_parts(pre_first.astype(jnp.float32))
    act_one = act_one.astype(jnp.bfloat16)
    extended_two = pad_sides(with_halo(grad_two, (("gx", 0),), 1))
    stacked_two = stack_taps(extended_two, -1, z_cells)
    grad_act = back_data(stacked_two, full_second, shape)
    extended_act = pad_sides(with_halo(act_one, (("gx", 0),), 1))
    filt_two = filter_from_inputs(stack_taps(extended_act, 1, z_cells), grad_two, shape)
    owned_two = lax.psum_scatter(filt_two * grad_scale, "gx", scatter_dimension=0, tiled=True)
    grad_one = (grad_act * slope_one).astype(jnp.bfloat16)
    extended_one = pad_sides(with_halo(grad_one, (("gx", 0),), 1))
    stacked_one = stack_taps(extended_one, -1, z_cells)
    grad_in = back_data(stacked_one, full_first, shape).astype(jnp.bfloat16)
    extended_in = pad_sides(with_halo(inputs, (("gx", 0),), 1))
    filt_one = filter_from_inputs(stack_taps(extended_in, 1, z_cells), grad_one, shape)
    owned_one = lax.psum_scatter(filt_one * grad_scale, "gx", scatter_dimension=0, tiled=True)
    return (grad_in, owned_one, owned_two)


MESH = pl.DeviceIdType.MESH
sub = 8


def shift_z(block, shift):
    if shift == 0:
        return block
    cells = block.shape[0]
    row = lax.broadcasted_iota(jnp.int32, block.shape, 0)
    edge = 0 if shift > 0 else cells - 1
    return jnp.where(row == edge, 0.0, pltpu.roll(block, shift % cells, 0))


def kernel(
    n, go_in, xin_in, p1_in, p2_in, f1_in, f2_in, gin, own1, own2,
    go, xin, p1, p2,
    fbuf, wbuf, gext, abuf, ahalo, sat, turned, gcat, slope, part, s1, r1, s2, r2, s3, r3, rg, s4, r4,
    load, halo_s, halo_r, sent, line_r, relay_r, cross_r, core_r, late_r,
    rs1_r, rs2_r, rs3_r, rsg_r,
):
    xs, ys, zs, ch = go.shape
    units = f1_in.shape[0]
    hi = n // 4
    grad_scale = 1.0 / math.sqrt(xs * n * ys * zs)
    group, me = lax.axis_index("groups"), lax.axis_index("gx")
    core = me % 2
    mid = (me // 2) % 2
    top = me // 4
    partner = me + 1 - 2 * core
    across = me + 2 - 4 * mid
    lead = core == group
    follower = jnp.logical_not(lead)
    upper = top // ((hi + 1) // 2)
    room = top + upper * (hi - 1 - 2 * top)
    place = top + (1 - upper) * (hi - 1 - 2 * top)
    near_side = far = hi // 2
    gate = far - 1 + upper
    outer = top != gate
    gate_slot = (top - gate - 1) % near_side

    def owner(t, m, c):
        return (t * 2 + m) * 2 + c

    def chunk(t, m, c):
        return pl.ds(owner(t, m, c) * units, units)

    def at_least(value, bound):
        return 1 - 1 // (1 + value // bound)

    def near(k):
        both = at_least(2 * room, k)
        step = both * ((k + 1) // 2) + (1 - both) * (k - room)
        return top + (1 - 2 * upper) * (1 - 2 * both * ((k + 1) % 2)) * step

    def from_far(i):
        return (1 - upper) * (hi - 1 - i) + upper * i

    def same_side(k):
        return upper * far + (top - upper * far + k) % near_side

    def ranked(j):
        return (at_least(j, 1) - at_least(j, 2)) * (hi - 1) + at_least(j, 2) * (j - 1)

    rank = at_least(top, 1) * (top + 1) - at_least(top, hi - 1) * (hi - 1)

    def low_peer(i):
        return ranked(i + at_least(i + 1, rank + 1))

    def remote(src, dst, send, recv, target, plane):
        return pltpu.make_async_remote_copy(
            src_ref=src, dst_ref=dst, send_sem=send, recv_sem=recv,
            device_id=(plane, target), device_id_type=MESH,
        )

    def push(src, dst, count, recv, target, plane=group):
        remote(src, dst, sent.at[count], recv, target, plane).start()

    def arrive(dst, recv):
        remote(dst, dst, sent.at[0], recv, partner, group).wait_recv()

    def pieces(f, count):
        return fbuf.at[f, pl.ds(0, count * units)]

    barrier = pltpu.get_barrier_semaphore()
    peers = [partner, across, lax.rem(me + 1, n), lax.rem(me + n - 1, n)]
    peers += [owner(near(k), mid, core) for k in range(1, hi)]
    for peer in peers:
        pl.semaphore_signal(barrier, inc=1, device_id=(group, peer), device_id_type=MESH)
    pl.semaphore_signal(barrier, inc=1, device_id=(1 - group, me), device_id_type=MESH)

    own_chunk = chunk(top, mid, core)
    loads = [
        pltpu.make_async_copy(src, dst, load.at[i])
        for i, (src, dst) in enumerate(
            (
                (f2_in, fbuf.at[0, own_chunk]), (p2_in, p2), (go_in, go), (p1_in, p1),
                (xin_in, xin), (f1_in, fbuf.at[1, own_chunk]),
            )
        )
    ]
    for copy in loads:
        copy.start()

    for f in range(2):
        for x in range(xs + 2):
            for y in (0, ys + 1):
                gext[f, x, y] = jnp.zeros((zs, ch), jnp.bfloat16)
                gcat[f, x, y] = jnp.zeros((zs, 3 * ch), jnp.bfloat16)

    for x in range(xs + 2):
        for y in (0, ys + 1):
            turned[x, :, y * zs : (y + 1) * zs] = jnp.zeros((ch, zs), jnp.bfloat16)

    def mine(f):
        return fbuf.at[f, own_chunk]

    def to_partner(f, got):
        push(got, got, 3 * f, core_r.at[f], partner)

    def cross(f, got, recv):
        push(got, got, 4 + f, recv, me, 1 - group)
        to_partner(f, got)

    def first_own():
        push(mine(0), mine(0), 0, relay_r.at[top], across)

        @pl.when(lead)
        def _():
            for k in range(hi - 1, 0, -1):
                push(mine(0), mine(0), 4, line_r.at[top], owner(near(k), mid, core))

        to_partner(0, mine(0))

    def first_side():
        got = fbuf.at[0, chunk(top, 1 - mid, core)]
        arrive(got, relay_r.at[top])
        to_partner(0, got)

    def first_line():
        @pl.when(lead)
        def _():
            for k in range(1, hi):
                t = near(k)
                got = fbuf.at[0, chunk(t, mid, core)]
                arrive(got, line_r.at[t])
                push(got, got, 4, relay_r.at[t], across)
                cross(0, got, cross_r.at[mid * hi + t])

    def first_relay():
        @pl.when(lead)
        def _():
            for k in range(1, hi):
                t = near(k)
                got = fbuf.at[0, chunk(t, 1 - mid, core)]
                arrive(got, relay_r.at[t])
                cross(0, got, cross_r.at[(1 - mid) * hi + t])

    def first_follow():
        @pl.when(follower)
        def _():
            for side in range(2):
                which = 1 - mid if side else mid
                for k in range(1, hi):
                    t = near(k)
                    got = fbuf.at[0, chunk(t, which, core)]
                    arrive(got, cross_r.at[which * hi + t])
                    to_partner(0, got)

    def late_own():
        to_partner(1, mine(1))

        @pl.when(lead)
        def _():
            push(mine(1), mine(1), 5, late_r.at[0], across)

    def late_spread():
        @pl.when(lead)
        def _():
            for k in range(hi - 1, 0, -1):
                push(mine(1), mine(1), 5, late_r.at[1], owner(near(k), mid, core))

    def late_line():
        @pl.when(lead)
        def _():
            arrive(pieces(1, hi - 1), late_r.at[1])
            for k in range(1, hi):
                got = fbuf.at[1, chunk(near(k), mid, core)]
                push(got, got, 5, late_r.at[2], across)
                cross(1, got, late_r.at[3])

    def late_relay():
        @pl.when(lead)
        def _():
            arrive(mine(1), late_r.at[0])
            arrive(pieces(1, hi - 1), late_r.at[2])
            for k in range(hi):
                t = near(k) if k else top
                cross(1, fbuf.at[1, chunk(t, 1 - mid, core)], late_r.at[3])

    def late_follow():
        @pl.when(follower)
        def _():
            arrive(pieces(1, 2 * hi - 1), late_r.at[3])
            to_partner(1, fbuf.at[1, chunk(top, 1 - mid, core)])
            for k in range(1, hi):
                for m in range(2):
                    to_partner(1, fbuf.at[1, chunk(near(k), m, core)])

    def gather_core(f):
        arrive(pieces(f, 2 * hi), core_r.at[f])
        taps = 3 * ch // sub
        for ab in range(9):
            rows = fbuf[f, ab * taps : (ab + 1) * taps].astype(jnp.float32)
            wbuf[f, :, ab * ch : (ab + 1) * ch] = rows.reshape(3 * ch, ch).astype(jnp.bfloat16)

    def halo_copy(h, first, last, low, high):
        to_left = remote(
            first, high, halo_s.at[0], halo_r.at[h, 1], lax.rem(me + n - 1, n), group
        )
        to_right = remote(
            last, low, halo_s.at[1], halo_r.at[h, 0], lax.rem(me + 1, n), group
        )

        @pl.when(me > 0)
        def _():
            to_left.start()

        @pl.when(me < n - 1)
        def _():
            to_right.start()

        return low, high, h

    def halo_wait(halo):
        low, high, h = halo

        @pl.when(me > 0)
        def _():
            arrive(low, halo_r.at[h, 0])

        @pl.when(me == 0)
        def _():
            low[...] = jnp.zeros(low.shape, low.dtype)

        @pl.when(me < n - 1)
        def _():
            arrive(high, halo_r.at[h, 1])

        @pl.when(me == n - 1)
        def _():
            high[...] = jnp.zeros(high.shape, high.dtype)

    def grad_halo(f):
        inner = pl.ds(1, ys)
        return halo_copy(
            f, gext.at[f, 1, inner], gext.at[f, xs, inner],
            gext.at[f, 0, inner], gext.at[f, xs + 1, inner],
        )

    def saved_halo(h, block):
        return halo_copy(h, block.at[0], block.at[xs - 1], ahalo.at[0], ahalo.at[1])

    def keep_shifts(f, x, y, value):
        for c in (-1, 0, 1):
            gcat[f, x + 1, y + 1, :, (c + 1) * ch : (c + 2) * ch] = shift_z(value, c).astype(
                jnp.bfloat16
            )

    def keep_grad(f, x, y, value):
        gext[f, x + 1, y + 1] = value.astype(jnp.bfloat16)
        keep_shifts(f, x, y, value)

    def halo_shifts(f):
        for x in (-1, xs):
            for y in range(ys):
                keep_shifts(f, x, y, gext[f, x + 1, y + 1].astype(jnp.float32))

    def turn(layer, block):
        for y in range(ys):
            sat[0, layer, :, y * zs : (y + 1) * zs] = block[y].T

    def turn_input(layer, block):
        for y in range(ys):
            turned[layer, :, (y + 1) * zs : (y + 2) * zs] = block[y].T

    per = ch // sub

    def filter_terms(s, a):
        lhs = jnp.concatenate([sat[s, x] for x in range(xs)], axis=1)
        for b in (-1, 0, 1):
            rhs = gcat[s, pl.ds(2 - a, xs), 1 - b : 1 - b + ys].reshape(xs * ys * zs, 3 * ch)
            out = jnp.dot(lhs, rhs, preferred_element_type=jnp.float32)
            for c in range(3):
                part[s, pl.ds((9 * a + 3 * (b + 1) + c) * per, per)] = out[
                    :, c * ch : (c + 1) * ch
                ].reshape(per, sub, ch)

    def filter_terms_dense(s, a):
        lhs = jnp.concatenate(
            [
                jnp.concatenate(
                    [turned[x + a, :, b * zs : (b + ys) * zs] for x in range(xs)], axis=1
                )
                for b in range(3)
            ],
            axis=0,
        )
        rhs = gcat[s, 1 : xs + 1, 1 : ys + 1].reshape(xs * ys * zs, 3 * ch)
        out = jnp.dot(lhs, rhs, preferred_element_type=jnp.float32)
        for b in range(3):
            for c in range(3):
                part[s, pl.ds((9 * a + 3 * b + c) * per, per)] = out[
                    b * ch : (b + 1) * ch, c * ch : (c + 1) * ch
                ].reshape(per, sub, ch)

    def side_of(j):
        return mid if j else 1 - mid

    def scatter_core(s, t):
        for j in range(2):
            s1[s, t, j] = part[s, chunk(t, side_of(j), 1 - core)].astype(jnp.bfloat16)
            if s:
                push(s1.at[s, t, j], r1.at[s, t, j], 1 + s, rs1_r.at[s, hi if j else t], partner)
        if not s:
            push(s1.at[s, t], r1.at[s, t], 1 + s, rs1_r.at[s, t], partner)

    def terms_far():
        for j in range(3):
            filter_terms(0, (1 - upper) * (2 - j) + upper * j)
            for i in range(j * hi // 3, (j + 1) * hi // 3):
                scatter_core(0, from_far(i))

    def terms_ranked():
        ready, left_over = [], [0, hi - 1, *range(1, hi - 1)]
        for a in (0, 2, 1):
            filter_terms_dense(1, a)
            ready.append(a)
            for t in list(left_over):
                if all(block in ready for block in range(3 * t // hi, -(-3 * (t + 1) // hi))):
                    left_over.remove(t)
                    scatter_core(1, t)

    def cell(t, j):
        return chunk(t, side_of(j), core)

    def pair_sum(t):
        arrive(r1.at[0, t], rs1_r.at[0, t])
        return [part[0, cell(t, j)] + r1[0, t, j].astype(jnp.float32) for j in range(2)]

    def line_send(t, values, dst, recv, target):
        for j in range(2):
            s3[t, j] = values[j].astype(jnp.bfloat16)
        push(s3.at[t], dst, 1, recv, owner(target, mid, core))

    def line_out():
        for i in range(far):
            t = from_far(i)
            values = pair_sum(t)

            @pl.when(outer)
            def _():
                line_send(t, values, rg.at[i, gate_slot], rsg_r.at[0, i], gate)

            @pl.when(jnp.logical_not(outer))
            def _():
                for j in range(2):
                    part[0, cell(t, j)] = values[j]

        for k in range(1, near_side):
            t = same_side(k)
            line_send(t, pair_sum(t), r3.at[k - 1], rs3_r.at[0], t)

    def line_gate(steps):
        @pl.when(jnp.logical_not(outer))
        def _():
            for i in steps:
                t = from_far(i)
                arrive(rg.at[i, pl.ds(0, near_side - 1)], rsg_r.at[0, i])
                values = [part[0, cell(t, j)] for j in range(2)]
                for k in range(near_side - 1):
                    values = [values[j] + rg[i, k, j].astype(jnp.float32) for j in range(2)]
                line_send(t, values, r3.at[near_side - 1], rs3_r.at[0], t)

    def line_end():
        values = pair_sum(top)
        arrive(r3, rs3_r.at[0])
        for k in range(near_side):
            values = [values[j] + r3[k, j].astype(jnp.float32) for j in range(2)]
        part[0, own_chunk] = values[1]
        s2[0, 0] = values[0].astype(jnp.bfloat16)
        push(s2.at[0, 0], r2.at[0, 0], 1, rs2_r.at[0, 0], across)

    def line_store():
        arrive(r2.at[0, 0], rs2_r.at[0, 0])
        own2[...] = (part[0, own_chunk] + r2[0, 0].astype(jnp.float32)) * grad_scale

    def side_out(steps):
        for i in steps:
            t = low_peer(i) if i < hi - 1 else top
            arrive(r1.at[1, t, 0], rs1_r.at[1, t])
            s2[1, t] = (part[1, cell(t, 0)] + r1[1, t, 0].astype(jnp.float32)).astype(
                jnp.bfloat16
            )
            push(s2.at[1, t], r2.at[1, t], 2, rs2_r.at[1, t], across)

    def total(t):
        arrive(r2.at[1, t], rs2_r.at[1, t])
        return (
            part[1, cell(t, 1)]
            + r1[1, t, 1].astype(jnp.float32)
            + r2[1, t].astype(jnp.float32)
        )

    def send_last(t, value, dst, recv, target):
        s4[t] = value.astype(jnp.bfloat16)
        push(s4.at[t], dst, 2, recv, owner(target, mid, core))

    def side_line(steps):
        if 0 in steps:
            arrive(fbuf.at[0, pl.ds(0, hi * units)], rs1_r.at[1, hi])
        for i in steps:
            t = low_peer(i)
            send_last(t, total(t), r4.at[top - at_least(top, t + 1)], rs3_r.at[1], t)

    def side_store():
        value = total(top)
        arrive(r4, rs3_r.at[1])
        for k in range(hi - 1):
            value = value + r4[k].astype(jnp.float32)
        own1[...] = value * grad_scale

    def layer_back(f, x):
        lhs = jnp.concatenate(
            [
                gext[f, x + 1 - a, 1 - b : 1 - b + ys].reshape(ys * zs, ch)
                for a in (-1, 0, 1)
                for b in (-1, 0, 1)
            ],
            axis=1,
        )
        wide = lax.dot_general(
            lhs, wbuf[f], (((1,), (1,)), ((), ())), preferred_element_type=jnp.float32
        )
        rows = []
        for y in range(ys):
            block = wide[y * zs : (y + 1) * zs]
            rows.append(
                shift_z(block[:, :ch], -1) + block[:, ch : 2 * ch] + shift_z(block[:, 2 * ch :], 1)
            )
        return rows

    pl.semaphore_wait(barrier, len(peers) + 1)
    loads[0].wait()
    first_own()
    loads[1].wait()
    loads[2].wait()

    @pl.loop(0, xs * ys)
    def _(i):
        x, y = i // ys, i % ys
        _, slope_two = gelu_parts(p2[x, y].astype(jnp.float32))
        keep_grad(0, x, y, go[x, y].astype(jnp.float32) * slope_two)

    halo_two = grad_halo(0)
    loads[3].wait()

    @pl.loop(0, xs * ys)
    def _(i):
        x, y = i // ys, i % ys
        act, slope_one = gelu_parts(p1[x, y].astype(jnp.float32))
        abuf[x, y] = act.astype(jnp.bfloat16)
        slope[x, y] = slope_one

    loads[4].wait()
    for x in range(xs):
        turn(x, abuf[x])
        turn_input(x + 1, xin[x])
    loads[5].wait()
    first_line()
    first_side()
    halo_wait(halo_two)
    halo_shifts(0)
    late_own()
    late_spread()
    terms_far()
    first_relay()
    halo_in = saved_halo(2, xin)
    line_out()
    late_line()
    first_follow()
    gather_core(0)
    for x in range(xs):
        for y, value in enumerate(layer_back(0, x)):
            keep_grad(1, x, y, value * slope[x, y])
    halo_one = grad_halo(1)
    line_gate((0,))
    late_relay()
    halo_wait(halo_in)
    turn_input(0, ahalo[0])
    turn_input(xs + 1, ahalo[1])
    terms_ranked()
    line_gate(range(1, far))
    side_out(range(hi))
    late_follow()
    side_line(range(1))
    halo_wait(halo_one)
    gather_core(1)
    for x in range(xs):
        for y, value in enumerate(layer_back(1, x)):
            gin[x, y] = value.astype(jnp.bfloat16)
    side_line(range(1, hi - 2))
    line_end()
    side_line(range(hi - 2, hi - 1))
    line_store()
    side_store()

    def left(count, send):
        remote(pieces(0, count), pieces(0, count), send, core_r.at[0], partner, group).wait_send()

    for i, count in enumerate((2 * hi + 1, 4 * hi - 1, 4 * hi - 1, 2 * hi)):
        left(count, sent.at[i])

    @pl.when(lead)
    def _():
        left(4 * hi - 4, sent.at[4])
        left(4 * hi - 2, sent.at[5])

    layers = gext.at[0, pl.ds(0, 3), pl.ds(1, ys)]

    @pl.when(me > 0)
    def _():
        remote(layers, layers, halo_s.at[0], core_r.at[0], partner, group).wait_send()

    @pl.when(me < n - 1)
    def _():
        remote(layers, layers, halo_s.at[1], core_r.at[0], partner, group).wait_send()


def store_kernel(*refs):
    count = (len(refs) - 1) // 2
    copies = [
        pltpu.make_async_copy(refs[i], refs[count + i], refs[-1].at[i]) for i in range(count)
    ]
    for copy in copies:
        copy.start()
    for copy in copies:
        copy.wait()


def store_out(*results):
    return pl.pallas_call(
        store_kernel,
        out_shape=tuple(jax.ShapeDtypeStruct(r.shape, r.dtype) for r in results),
        in_specs=[pl.BlockSpec(memory_space=pltpu.VMEM)] * len(results),
        out_specs=[pl.BlockSpec(memory_space=pl.ANY)] * len(results),
        scratch_shapes=[pltpu.SemaphoreType.DMA((len(results),))],
    )(*(pltpu.with_memory_space_constraint(r, pltpu.VMEM) for r in results))


def fused(grad_out, inputs, pre_first, pre_second, filter_first, filter_second):
    n = lax.axis_size("gx")
    xs, ys, zs, ch = grad_out.shape
    rows = filter_first.shape[0]
    if rows % sub or n % 8 or n < 16 or lax.axis_size("groups") != 2:
        return on_device(grad_out, inputs, pre_first, pre_second, filter_first, filter_second)
    units, hi, bf = rows // sub, n // 4, jnp.bfloat16
    dma = pltpu.SemaphoreType.DMA
    piece = (units, sub, ch)
    block = pltpu.VMEM((xs, ys, zs, ch), bf)
    gin, own1, own2 = pl.pallas_call(
        functools.partial(kernel, n),
        out_shape=(
            pltpu.VMEM(grad_out.shape, bf),
            pltpu.VMEM(piece, jnp.float32),
            pltpu.VMEM(piece, jnp.float32),
        ),
        in_specs=[pl.BlockSpec(memory_space=pl.ANY)] * 6,
        out_specs=[pl.BlockSpec(memory_space=pltpu.VMEM)] * 3,
        scratch_shapes=[
            block, block, block, block,
            pltpu.VMEM((2, n * units, sub, ch), bf),
            pltpu.VMEM((2, 3 * ch, 9 * ch), bf),
            pltpu.VMEM((2, xs + 2, ys + 2, zs, ch), bf),
            block,
            pltpu.VMEM((2, ys, zs, ch), bf),
            pltpu.VMEM((1, xs, ch, ys * zs), bf),
            pltpu.VMEM((xs + 2, ch, (ys + 2) * zs), bf),
            pltpu.VMEM((2, xs + 2, ys + 2, zs, 3 * ch), bf),
            pltpu.VMEM((xs, ys, zs, ch), jnp.float32),
            pltpu.VMEM((2, n * units, sub, ch), jnp.float32),
            pltpu.VMEM((2, hi, 2) + piece, bf),
            pltpu.VMEM((2, hi, 2) + piece, bf),
            pltpu.VMEM((2, hi) + piece, bf),
            pltpu.VMEM((2, hi) + piece, bf),
            pltpu.VMEM((hi, 2) + piece, bf),
            pltpu.VMEM((hi // 2, 2) + piece, bf),
            pltpu.VMEM((hi // 2, hi // 2, 2) + piece, bf),
            pltpu.VMEM((hi,) + piece, bf),
            pltpu.VMEM((hi - 1,) + piece, bf),
            dma((6,)), dma((2,)), dma((3, 2)), dma((6,)),
            dma((hi,)), dma((hi,)), dma((2 * hi,)), dma((2,)), dma((4,)),
            dma((2, hi + 1)), dma((2, hi)), dma((2,)), dma((1, hi // 2)),
        ],
        compiler_params=pltpu.CompilerParams(collective_id=0, has_side_effects=True),
    )(
        grad_out, inputs, pre_first, pre_second,
        filter_first.reshape(piece), filter_second.reshape(piece),
    )
    gin, own1, own2 = store_out(gin, own1, own2)
    return gin, own1.reshape(rows, ch), own2.reshape(rows, ch)


def solution(mesh):
    return jax.shard_map(
        fused,
        mesh=mesh,
        in_specs=(
            P(("groups", "gx"), None, None, None),
            P(("groups", "gx"), None, None, None),
            P(("groups", "gx"), None, None, None),
            P(("groups", "gx"), None, None, None),
            P("gx", None),
            P("gx", None),
        ),
        out_specs=(P(("groups", "gx"), None, None, None), P("gx", "groups"), P("gx", "groups")),
        check_vma=False,
    )
```
